128 devices in a mesh: slot: 32 (over y, z, core), hid: 4 (over x).
Axes of the slice: x: 4, y: 4, z: 4, core: 2. Of those that a mesh axis runs over, the one named last changes fastest.
Arguments:
- master: float32 [16, 3, 4, 393216], P(None, None, 'hid', 'slot'), may hold values from -0.125 to 0.125
- first_moment: float32 [16, 3, 4, 393216], P(None, None, 'hid', 'slot'), may hold values from -0.3 to 0.3
- second_moment: float32 [16, 3, 4, 393216], P(None, None, 'hid', 'slot'), may hold values from 0.0001 to 0.01
- slot_weights: bfloat16 [32, 3, 768, 2048], P('slot', None, 'hid'), may hold values from -0.125 to 0.125
- back_rows: bfloat16 [32, 1024, 2048], P('slot'), may hold values from -6 to 6
- readout: bfloat16 [32, 1024, 2048], P('slot'), may hold values from -0.25 to 0.25
- ref_logratio: float32 [32, 1024], P('slot'), may hold values from -9 to 0
- labels: int32 [32, 1024], P('slot'), may hold values 0 or 1
- place_cur: int32 [32], replicated, may hold values from 0 to 15, as said below
- place_next: int32 [32], replicated, may hold values from 0 to 15, as said below
- fwd_rows: bfloat16 [8192, 2048], P('slot', 'hid'), may hold values from -6 to 6
- routes: int32 [8192, 1], P('slot'), may hold values from 0 to 31; in each aligned block of 256 rows (0 to 255, 256 to 511, ...) at most 16 rows name the same one
Outputs:
- out_rows: bfloat16 [8192, 2048], P('slot', 'hid')
- new_master: float32 [16, 3, 4, 393216], P(None, None, 'hid', 'slot')
- new_first: float32 [16, 3, 4, 393216], P(None, None, 'hid', 'slot')
- new_second: float32 [16, 3, 4, 393216], P(None, None, 'hid', 'slot')
The draws below stay inside these ranges and needn't reach their ends.
Inputs may be any that keep to these rules, and one draw needn't show every extreme that they name: `place_cur`: every expert 0 to 15 is held by at least one slot. `place_next`: every expert 0 to 15 is held by at least one slot. `routes`: the rows of one slot name any one slot at most 16 times, a bound that some block reaches.
All inputs are finite; a program needn't handle non-finite values. No bound on the sum of `labels` on one device may be relied on, other than what follows from the above.
Results may differ from the reference program's by a relative error of at most 0.008.
Values may be sent and summed in bfloat16 or wider, within the bound.
No kernel may reach another device: no remote copies, remote signals or barrier semaphores. Data moves between devices by JAX's collectives and lax.ppermute only.
A program may use at most 128 MiB of HBM per device.

```python
import math
import jax
import jax.numpy as jnp
import numpy as np
from jax import lax

D = 2048
FF = 768
ROWS_B = 1024
ROWS_F = 256
SLOTS = 32
EXPERTS = 16
CAP = 16
N_HID = 4


def placement_draw(key):
    spare_slots = SLOTS - EXPERTS
    key_list = jax.random.split(key, 4)
    first_pick = jax.random.randint(key_list[0], (spare_slots,), 0, EXPERTS)
    second_pick = jax.random.randint(key_list[1], (spare_slots,), 0, EXPERTS)
    relabel = jax.random.permutation(key_list[2], EXPERTS)
    chosen = relabel[jnp.minimum(first_pick, second_pick)].astype(jnp.int32)
    listed = jnp.concatenate([jnp.arange(EXPERTS, dtype=jnp.int32), chosen])
    shuffle = jax.random.permutation(key_list[3], SLOTS)
    return listed[shuffle].astype(jnp.int32)


def draw_place_cur(key, part):
    return placement_draw(jax.random.fold_in(key, 11))


def draw_place_next(key, part):
    return placement_draw(jax.random.fold_in(key, 23))


def draw_ref_logratio(key, part):
    inner_key = jax.random.fold_in(key, 37)
    ramp = 1.0 + 2.0 * jnp.arange(SLOTS, dtype=jnp.float32)[:, None] / max(SLOTS - 1, 1)
    rough = jax.random.uniform(inner_key, (SLOTS, ROWS_B), jnp.float32, 0.5, 1.5)
    return (-0.5 * ramp * rough).astype(jnp.float32)


def plant(result, stream_key, smallest, high):
    shape = result.shape
    spot = [jax.random.randint(jax.random.fold_in(stream_key, axis), (), 0, shape[axis]) for axis in range(len(shape))]
    result = result.at[tuple(spot)].set(smallest)
    longest = shape.index(max(shape))
    spot[longest] = (spot[longest] + 1) % shape[longest]
    return result.at[tuple(spot)].set(high)


def shard_levels(rng, extent, cuts, least, top_value):
    factor_of, own = 1.0, jax.random.fold_in(rng, 6)
    for position, parts in cuts:
        steps = jnp.exp(jax.random.uniform(jax.random.fold_in(own, position), (parts,), jnp.float32, least / len(cuts), top_value / len(cuts)))
        factor_of = factor_of * jnp.repeat(steps, extent[position] // parts).reshape([-1 if axis == position else 1 for axis in range(len(extent))])
    return factor_of


def shared_out(rng, own, number, rows, amount, top, most, skew):
    sequence = jax.random.permutation(rng, amount)
    crowded, usual = shares(amount, rows * top, most, skew, True), shares(amount, rows * top, most, skew, False)
    places = jnp.arange(amount)

    def named(sizes, turn):
        used = int((sizes > 0).sum())
        fixed = max(1, used // 4)
        shifted = fixed + (places - fixed + turn * (used - fixed)) % max(1, amount - fixed)
        return jnp.zeros((amount,), jnp.int32).at[sequence[jnp.where(places < fixed, places, shifted)]].set(jnp.asarray(sizes, jnp.int32))

    sizes = jnp.where(number % 4 == 0, named(crowded, number // 4), named(usual, number - number // 4 - 1))
    mixed = jax.random.permutation(jax.random.fold_in(own, 3), amount)
    giver, receiver = mixed[0:amount // 2 * 2:2], mixed[1:amount // 2 * 2:2]
    margin = jnp.minimum(sizes[giver] - 1, most - sizes[receiver]) // 2
    margin = jnp.where((giver == sequence[0]) | (receiver == sequence[0]) | (sizes[receiver] == 0), 0, jnp.maximum(margin, 0))
    shifted = jax.random.randint(jax.random.fold_in(own, 4), (amount // 2,), 0, 1 << 20) % (margin + 1)
    sizes = sizes.at[giver].add(-shifted).at[receiver].add(shifted)
    members = jnp.searchsorted(jnp.cumsum(sizes), jnp.arange(rows * top), side="right").astype(jnp.int32)
    table = members.reshape(top, rows).T
    table = table[jax.random.permutation(jax.random.fold_in(own, 1), rows)]
    turn = jax.random.randint(jax.random.fold_in(own, 2), (rows, 1), 0, top)
    return jnp.take_along_axis(table, (jnp.arange(top)[None, :] + turn) % top, axis=1)


def shares(number_of, total, bound, lean, full):
    loads = [(1 << 20) // math.isqrt(grade ** lean) + 1 for grade in range(1, number_of + 1)]
    largest = bound if full else min(bound, max(-(-total // number_of), total * loads[0] // sum(loads)))
    least = 1 if total - largest >= number_of - 1 else 0
    given, spare = [largest] + [least] * (number_of - 1), total - largest - least * (number_of - 1)
    while spare > 0:
        candidates = [i for i in range(1, number_of) if given[i] < largest] or [i for i in range(1, number_of) if given[i] < bound]
        whole, left = sum([loads[i] for i in candidates]), spare
        for i in candidates:
            extra = min(bound - given[i], max(1, left * loads[i] // whole), spare)
            given[i] = given[i] + extra
            spare = spare - extra
    return np.array(given)


def bell_draw(own_key, dims, width, reach, shards=(), held_as=jnp.bfloat16):
    level = shard_levels(own_key, dims, shards, -0.22, 0.18) if shards else 1.0
    result = jax.random.normal(own_key, dims, jnp.float32) * width * level
    return jnp.minimum(jnp.maximum(result, -reach), reach).astype(held_as)


def setup_inputs(seed: int = 0) -> dict:
    streams_of = jax.random.split(jax.random.key(seed), 13)
    master = bell_draw(streams_of[0], (EXPERTS, 3, N_HID, FF * D // N_HID), D ** -0.5, 0.125, ((2, 4), (3, 32)), jnp.float32)
    first_moment = bell_draw(streams_of[1], (EXPERTS, 3, N_HID, FF * D // N_HID), 0.05, 0.3, ((2, 4), (3, 32)), jnp.float32)
    second_moment = jnp.clip(jnp.exp(math.log(0.01) - 4.6051702 * jax.random.uniform(streams_of[2], (EXPERTS, 3, N_HID, FF * D // N_HID), jnp.float32) ** shard_levels(streams_of[2], (EXPERTS, 3, N_HID, FF * D // N_HID), ((2, 4), (3, 32)), -0.2, 0.2)), 0.0001, 0.01)
    slot_weights = bell_draw(streams_of[3], (SLOTS, 3, FF, D), D ** -0.5, 0.125, ((0, 32), (2, 4)))
    back_rows = bell_draw(streams_of[4], (SLOTS, ROWS_B, D), 1.0, 6.0, ((0, 32),))
    readout = bell_draw(streams_of[5], (SLOTS, ROWS_B, D), (D // 4) ** -0.5, 0.25, ((0, 32),))
    ref_logratio = draw_ref_logratio(jax.random.fold_in(streams_of[12], 71), 0)
    labels = plant((jax.random.randint(streams_of[7], (SLOTS, ROWS_B), 0, 2) < 1).astype(jnp.int32), jax.random.fold_in(streams_of[7], 1), 0, 1)
    place_cur = draw_place_cur(jax.random.fold_in(streams_of[12], 71), 0)
    place_next = draw_place_next(jax.random.fold_in(streams_of[12], 71), 0)
    fwd_rows = bell_draw(streams_of[10], (SLOTS * ROWS_F, D), 1.0, 6.0, ((0, 32), (1, 4)))
    routes_keys = jax.random.split(jax.random.fold_in(streams_of[11], 1), (SLOTS * ROWS_F) // ROWS_F)
    routes_turns = jax.random.permutation(jax.random.fold_in(streams_of[11], 3), (SLOTS * ROWS_F) // ROWS_F)
    routes = jax.vmap(lambda own, number: shared_out(jax.random.fold_in(streams_of[11], 2), own, number, ROWS_F, SLOTS, 1, CAP, 2))(routes_keys, routes_turns).reshape((SLOTS * ROWS_F, 1))
    return {"master": master, "first_moment": first_moment, "second_moment": second_moment, "slot_weights": slot_weights, "back_rows": back_rows, "readout": readout, "ref_logratio": ref_logratio, "labels": labels, "place_cur": place_cur, "place_next": place_next, "fwd_rows": fwd_rows, "routes": routes}


beta_kto = 1.0
desired_weight = 1.0
undesired_weight = 1.33
learn_rate = 0.004
decay_first = 0.9
decay_second = 0.999
correct_first = 0.9999734386011124
correct_second = 0.09520785288629043
adam_eps = 1e-08
weight_decay = 0.1

def expert_pass(inputs, weights):
    across = (((1,), (1,)), ((), ()))
    gate_vals = lax.dot_general(inputs, weights[0], across, preferred_element_type=jnp.float32)
    up_vals = lax.dot_general(inputs, weights[1], across, preferred_element_type=jnp.float32)
    hidden = (gate_vals * jax.nn.sigmoid(gate_vals) * up_vals).astype(jnp.bfloat16)
    produced = jnp.dot(hidden, weights[2], preferred_element_type=jnp.float32)
    return (gate_vals, up_vals, hidden, produced)

def kto_slope(scores, labels, center):
    sigma_v = jax.nn.sigmoid(beta_kto * (scores - center))
    signed = jnp.where(labels == 1, -desired_weight, undesired_weight)
    return beta_kto * sigma_v * (1.0 - sigma_v) * signed

def expert_grads(inputs, direction, weights, slope):
    gate_vals, up_vals, hidden, _ = expert_pass(inputs, weights)
    d_expert = (slope[:, None] * direction.astype(jnp.float32)).astype(jnp.bfloat16)
    d_hidden = lax.dot_general(d_expert, weights[2], (((1,), (1,)), ((), ())), preferred_element_type=jnp.float32)
    sigma_g = jax.nn.sigmoid(gate_vals)
    d_gate = (d_hidden * up_vals * sigma_g * (1.0 + gate_vals * (1.0 - sigma_g))).astype(jnp.bfloat16)
    d_up = (d_hidden * gate_vals * sigma_g).astype(jnp.bfloat16)
    contract = (((0,), (0,)), ((), ()))
    grad_gate = lax.dot_general(d_gate, inputs, contract, preferred_element_type=jnp.float32)
    grad_up = lax.dot_general(d_up, inputs, contract, preferred_element_type=jnp.float32)
    grad_down = lax.dot_general(hidden, d_expert, contract, preferred_element_type=jnp.float32)
    return jnp.stack([grad_gate, grad_up, grad_down])

def adamw_update(master, first_moment, second_moment, summed):
    new_first = decay_first * first_moment + (1.0 - decay_first) * summed
    new_second = decay_second * second_moment + (1.0 - decay_second) * summed * summed
    update = new_first / correct_first / (jnp.sqrt(new_second / correct_second) + adam_eps)
    new_master = master - learn_rate * (update + weight_decay * master)
    return (new_master, new_first, new_second)

def reference(master, first_moment, second_moment, slot_weights, back_rows, readout, ref_logratio, labels, place_cur, place_next, fwd_rows, routes):

    def policy_terms(packed):
        inputs, direction, weights = packed
        produced = expert_pass(inputs, weights)[3]
        return lax.optimization_barrier(jnp.sum(produced * direction.astype(jnp.float32), axis=1))
    policy = lax.map(policy_terms, (back_rows, readout, slot_weights))
    scores = policy - ref_logratio
    center = jnp.mean(scores)
    slope = kto_slope(scores, labels, center)

    def accumulate(running, packed):
        inputs, direction, weights, slope_row, expert_id = packed
        grads = expert_grads(inputs, direction, weights, slope_row)
        return (running.at[expert_id].add(grads), None)
    start_sum = jnp.zeros((EXPERTS, 3, FF, D), jnp.float32)
    summed, _ = lax.scan(accumulate, start_sum, (back_rows, readout, slot_weights, slope, place_cur))
    summed = summed.reshape(master.shape)
    new_master, new_first, new_second = adamw_update(master, first_moment, second_moment, summed)
    next_weights = new_master.astype(jnp.bfloat16).reshape(EXPERTS, 3, FF, D)[place_next]
    target = routes[:, 0].astype(jnp.int32)
    total_rows = target.shape[0]
    span = SLOTS * CAP
    sort_order = jnp.argsort(target, stable=True).astype(jnp.int32)
    sorted_rows = jnp.concatenate([fwd_rows[sort_order], jnp.zeros((span, D), jnp.bfloat16)], axis=0)
    counts = lax.optimization_barrier(jnp.sum((target[:, None] == jnp.arange(SLOTS, dtype=jnp.int32)[None, :]).astype(jnp.int32), axis=0))
    starts = (jnp.cumsum(counts) - counts).astype(jnp.int32)

    def apply_slot(packed):
        weights, start_at = packed
        block_rows = lax.dynamic_slice_in_dim(sorted_rows, start_at, span, 0)
        return expert_pass(block_rows, weights)[3].astype(jnp.bfloat16)
    results = lax.map(apply_slot, (next_weights, starts))
    sorted_target = target[sort_order]
    within = (jnp.arange(total_rows, dtype=jnp.int32) - starts[sorted_target]).astype(jnp.int32)
    ordered_out = results[sorted_target, within]
    out_rows = jnp.zeros((total_rows, D), jnp.bfloat16).at[sort_order].set(ordered_out)
    return (out_rows, new_master, new_first, new_second)
```

```python
import functools

import jax
import jax.numpy as jnp
from jax import lax
from jax.experimental import pallas as pl
from jax.experimental.pallas import tpu as pltpu
from jax.sharding import PartitionSpec as P

desired_weight = 1.0
undesired_weight = 1.33
learn_rate = 0.004
decay_first = 0.9
decay_second = 0.999
correct_first = 0.9999734386011124
correct_second = 0.09520785288629043
adam_eps = 1e-08
weight_decay = 0.1

BF = jnp.bfloat16
F32 = jnp.float32
NT = (((1,), (1,)), ((), ()))
LANES = 128


def dot(a, b, dims=(((1,), (0,)), ((), ()))):
    return lax.dot_general(a, b, dims, preferred_element_type=F32)


def swap_map(n):
    size = n * n
    row = lax.broadcasted_iota(jnp.int32, (size, size), 0)
    col = lax.broadcasted_iota(jnp.int32, (size, size), 1)
    hit = ((row % n) == (col // n)) & ((row // n) == (col % n))
    return jnp.where(hit, 1.0, 0.0).astype(BF)


def scores_kernel(x_ref, r_ref, w_ref, ref_ref, a_ref, b_ref, h_ref, part_ref):
    gate = dot(w_ref[0], x_ref[...], NT)
    up = dot(w_ref[1], x_ref[...], NT)
    dh = dot(w_ref[2], r_ref[...], NT)
    sigma = jax.nn.sigmoid(gate)
    hidden = (gate * sigma * up).astype(BF)
    h_ref[...] = hidden
    part_ref[...] = jnp.sum(hidden.astype(F32) * dh, axis=0, keepdims=True) - 0.25 * ref_ref[...]
    a_ref[...] = dh * up * sigma * (1.0 + gate * (1.0 - sigma))
    b_ref[...] = dh * gate * sigma


def scores_call(inputs, direction, weights, ref_logratio):
    rows, width = inputs.shape
    units = weights.shape[1]
    block = 256
    return pl.pallas_call(
        scores_kernel,
        grid=(rows // block,),
        in_specs=[
            pl.BlockSpec((block, width), lambda i: (i, 0)),
            pl.BlockSpec((block, width), lambda i: (i, 0)),
            pl.BlockSpec((3, units, width), lambda i: (0, 0, 0)),
            pl.BlockSpec((1, block), lambda i: (0, i)),
        ],
        out_specs=[
            pl.BlockSpec((units, block), lambda i: (0, i)),
            pl.BlockSpec((units, block), lambda i: (0, i)),
            pl.BlockSpec((units, block), lambda i: (0, i)),
            pl.BlockSpec((1, block), lambda i: (0, i)),
        ],
        out_shape=[
            jax.ShapeDtypeStruct((units, rows), F32),
            jax.ShapeDtypeStruct((units, rows), F32),
            jax.ShapeDtypeStruct((units, rows), BF),
            jax.ShapeDtypeStruct((1, rows), F32),
        ],
        cost_estimate=pl.CostEstimate(
            flops=6 * rows * width * units, bytes_accessed=14 << 20, transcendentals=rows * units
        ),
        name="scores",
    )(inputs, direction, weights, ref_logratio)


def grads_kernel(count, own_ref, parts_ref, lab_ref, *refs):
    terms = refs[:count]
    m_ref = refs[count]
    outs = refs[count + 1 : 2 * count + 1]
    lhs, held = refs[2 * count + 1 :]
    step = pl.program_id(0)
    units, rows = terms[0].shape
    wide = m_ref.shape[1]
    row_total = parts_ref.shape[0] // 4 * rows

    @pl.when(step == 0)
    def _():
        center = jnp.sum(parts_ref[...]) / row_total
        scores = jnp.sum(parts_ref[pl.ds(own_ref[0] * 4, 4)], axis=0)
        q = jax.nn.sigmoid(scores - center)
        slope = q * (1.0 - q) * jnp.where(lab_ref[...] == 1, -desired_weight, undesired_weight)
        for k in range(count):
            for i in range(rows // LANES):
                cols = slice(i * LANES, (i + 1) * LANES)
                lhs[k * units : (k + 1) * units, cols] = (
                    terms[k][:, cols].astype(F32) * slope[i : i + 1]
                ).astype(BF)

    held[:, pl.ds(pl.multiple_of(step * wide, wide), wide)] = dot(lhs[...], m_ref[...]).astype(BF)

    @pl.when(step == pl.num_programs(0) - 1)
    def _():
        swap = swap_map(16)
        for k in range(count):
            for pair in range(units // 32):
                halves = []
                for half in range(2):
                    base = k * units + (2 * pair + half) * 16
                    halves.append(
                        jnp.concatenate(
                            [
                                held[base : base + 16, j * LANES : (j + 1) * LANES]
                                for j in range(16)
                            ],
                            axis=0,
                        )
                    )
                both = dot(swap, jnp.concatenate(halves, axis=1)).astype(BF)
                outs[k][pair * 512 : pair * 512 + 256] = both[:, :LANES]
                outs[k][pair * 512 + 256 : pair * 512 + 512] = both[:, LANES:]


def grads_call(own, parts, labels, terms, right):
    count = len(terms)
    units, rows = terms[0].shape
    width = right.shape[1]
    wide = 512
    whole = lambda shape: pl.BlockSpec(shape, lambda i: (0,) * len(shape))
    return pl.pallas_call(
        functools.partial(grads_kernel, count),
        grid=(width // wide,),
        in_specs=[
            pl.BlockSpec(memory_space=pltpu.SMEM),
            whole(parts.shape),
            whole(labels.shape),
            *[whole(t.shape) for t in terms],
            pl.BlockSpec((rows, wide), lambda i: (0, i)),
        ],
        out_specs=[whole((units * 16, LANES))] * count,
        out_shape=[jax.ShapeDtypeStruct((units * 16, LANES), BF)] * count,
        scratch_shapes=[
            pltpu.VMEM((count * units, rows), BF),
            pltpu.VMEM((count * units, width), BF),
        ],
        cost_estimate=pl.CostEstimate(
            flops=2 * count * rows * width * units, bytes_accessed=6 << 20, transcendentals=rows
        ),
        name="grads%d" % count,
    )(own, parts, labels, *terms, right)


def adam_kernel(pc_ref, pn_ref, arr_ref, ms_ref, m1_ref, m2_ref, *refs):
    om_ref, o1_ref, o2_ref, pick_ref, total, fresh = refs[-6:]
    total[...] = jnp.zeros_like(total)
    for s in range(arr_ref.shape[0]):
        total[pc_ref[s]] += arr_ref[s].astype(F32)
    for e in range(total.shape[0]):
        grad = total[e]
        master = ms_ref[e, 0]
        new_first = decay_first * m1_ref[e, 0] + (1.0 - decay_first) * grad
        new_second = decay_second * m2_ref[e, 0] + (1.0 - decay_second) * grad * grad
        update = new_first / correct_first / (jnp.sqrt(new_second / correct_second) + adam_eps)
        new_master = master - learn_rate * (update + weight_decay * master)
        om_ref[e, 0] = new_master
        o1_ref[e, 0] = new_first
        o2_ref[e, 0] = new_second
        fresh[e] = new_master.astype(BF)
    for t in range(pick_ref.shape[0]):
        pick_ref[t] = fresh[pn_ref[t]]


def adam_call(which, place_cur, place_next, arrived, states, held):
    slots, lines, _ = arrived.shape
    experts = states[0].shape[0]
    block = 32
    state = pl.BlockSpec((experts, 1, block, LANES), lambda i: (0, which, i, 0))
    piece = pl.BlockSpec((slots, block, LANES), lambda i: (0, i, 0))
    smem = pl.BlockSpec(memory_space=pltpu.SMEM)
    extra = [] if held is None else list(held)
    return pl.pallas_call(
        adam_kernel,
        grid=(lines // block,),
        in_specs=[smem, smem, piece, state, state, state]
        + [pl.BlockSpec(memory_space=pl.ANY)] * len(extra),
        out_specs=[state, state, state, piece],
        out_shape=[jax.ShapeDtypeStruct(s.shape, F32) for s in states]
        + [jax.ShapeDtypeStruct(arrived.shape, BF)],
        scratch_shapes=[
            pltpu.VMEM((experts, block, LANES), F32),
            pltpu.VMEM((experts, block, LANES), BF),
        ],
        input_output_aliases={6 + i: i for i in range(len(extra))},
        cost_estimate=pl.CostEstimate(
            flops=20 * experts * lines * LANES, bytes_accessed=6 << 20, transcendentals=0
        ),
        name="adam%d" % which,
    )(place_cur, place_next, arrived, *states, *extra)


def to_matrix(src_ref, dst_ref):
    swap = swap_map(16)
    for pair in range(dst_ref.shape[0] // 32):
        base = pair * 512
        both = jnp.concatenate(
            [src_ref[base : base + 256], src_ref[base + 256 : base + 512]], axis=1
        )
        turned = dot(swap, both).astype(BF)
        for half in range(2):
            top = pair * 32 + half * 16
            for j in range(16):
                dst_ref[top : top + 16, j * LANES : (j + 1) * LANES] = turned[
                    j * 16 : (j + 1) * 16, half * LANES : (half + 1) * LANES
                ]


def project(q_ref, rows, mat):
    quarter = rows[0].shape[1]
    total = None
    for k in range(4):
        start = pl.multiple_of(q_ref[k] * quarter, quarter)
        term = dot(rows[k][...], mat[:, pl.ds(start, quarter)], NT)
        total = term if total is None else total + term
    return total


def gate_kernel(q_ref, w_ref, r0, r1, r2, r3, out_ref, mat):
    to_matrix(w_ref, mat)
    out_ref[...] = project(q_ref, (r0, r1, r2, r3), mat)


def up_kernel(q_ref, w_ref, r0, r1, r2, r3, gate_ref, out_ref, mat):
    to_matrix(w_ref, mat)
    up = project(q_ref, (r0, r1, r2, r3), mat)
    gate = gate_ref[...]
    out_ref[...] = (gate * jax.nn.sigmoid(gate) * up).astype(BF)


def project_call(quarters, packed, rows, gate):
    units = packed.shape[0] // 16
    count = rows[0].shape[0]
    width = rows[0].shape[1] * 4
    vmem = pl.BlockSpec(memory_space=pltpu.VMEM)
    extra = [] if gate is None else [gate]
    return pl.pallas_call(
        gate_kernel if gate is None else up_kernel,
        in_specs=[pl.BlockSpec(memory_space=pltpu.SMEM)] + [vmem] * (5 + len(extra)),
        out_specs=vmem,
        out_shape=jax.ShapeDtypeStruct((count, units), F32 if gate is None else BF),
        scratch_shapes=[pltpu.VMEM((units, width), BF)],
        cost_estimate=pl.CostEstimate(
            flops=2 * count * width * units, bytes_accessed=4 << 20, transcendentals=0
        ),
        name="gate" if gate is None else "up",
    )(quarters, packed, *rows, *extra)


def down_kernel(w_ref, hidden_ref, out_ref, mat):
    to_matrix(w_ref, mat)
    quarter = out_ref.shape[2]
    for k in range(4):
        out_ref[k] = dot(hidden_ref[...], mat[:, k * quarter : (k + 1) * quarter]).astype(BF)


def down_call(packed, hidden):
    count, units = hidden.shape
    width = 16 * LANES
    vmem = pl.BlockSpec(memory_space=pltpu.VMEM)
    return pl.pallas_call(
        down_kernel,
        in_specs=[vmem, vmem],
        out_specs=vmem,
        out_shape=jax.ShapeDtypeStruct((4, count, width // 4), BF),
        scratch_shapes=[pltpu.VMEM((units, width), BF)],
        cost_estimate=pl.CostEstimate(
            flops=2 * count * width * units, bytes_accessed=4 << 20, transcendentals=0
        ),
        name="down",
    )(packed, hidden)


def shards(
    master,
    first_moment,
    second_moment,
    slot_weights,
    back_rows,
    readout,
    ref_logratio,
    labels,
    place_cur,
    place_next,
    fwd_rows,
    routes,
):
    slot_count = lax.axis_size("slot")
    hid_count = lax.axis_size("hid")
    everyone = slot_count * hid_count
    slot_index = lax.axis_index("slot").astype(jnp.int32)
    hid_index = lax.axis_index("hid").astype(jnp.int32)
    rows = back_rows.shape[1]
    term_gate, term_up, hidden, part = scores_call(
        back_rows[0], readout[0], slot_weights[0], ref_logratio
    )
    part = jnp.broadcast_to(part.reshape(1, rows // LANES, LANES), (everyone, rows // LANES, LANES))
    parts = lax.all_to_all(part, ("slot", "hid"), split_axis=0, concat_axis=0, tiled=True)

    capacity = 2 * fwd_rows.shape[0] // slot_count
    quarter = fwd_rows.shape[1]
    target = routes[:, 0]
    target_map = (target[:, None] == jnp.arange(slot_count, dtype=jnp.int32)[None, :]).astype(BF)
    order = jnp.arange(fwd_rows.shape[0], dtype=jnp.int32)
    below = (order[:, None] > order[None, :]).astype(BF)
    earlier = jnp.dot(below, target_map, preferred_element_type=F32)
    position = jnp.sum(earlier * target_map.astype(F32), axis=1).astype(jnp.int32)
    slot_place = target * capacity + position
    place_map = (
        slot_place[None, :] == jnp.arange(slot_count * capacity, dtype=jnp.int32)[:, None]
    ).astype(BF)
    sent_rows = jnp.dot(place_map, fwd_rows, preferred_element_type=F32).astype(BF)
    sent_rows = sent_rows.reshape(slot_count, capacity, quarter)
    own_rows = lax.all_to_all(
        sent_rows, "slot", split_axis=0, concat_axis=0, tiled=True
    ).reshape(slot_count * capacity, quarter)
    pieces = [own_rows] + [
        lax.ppermute(own_rows, "hid", [(i, (i + k) % hid_count) for i in range(hid_count)])
        for k in range(1, hid_count)
    ]
    quarters = (hid_index - jnp.arange(hid_count, dtype=jnp.int32)) % hid_count

    own = slot_index.reshape(1)
    marks = labels.reshape(rows // LANES, LANES)
    (grad_down,) = grads_call(own, parts, marks, [hidden], readout[0])
    grad_gate, grad_up = grads_call(own, parts, marks, [term_gate, term_up], back_rows[0])
    lines = grad_down.shape[0] // slot_count

    def exchange(values):
        return lax.all_to_all(
            values.reshape(slot_count, lines, LANES), "slot", split_axis=0, concat_axis=0, tiled=True
        )

    got = {2: exchange(grad_down), 0: exchange(grad_gate), 1: exchange(grad_up)}
    shape = (master.shape[0], 3, lines, LANES)
    states = [v.reshape(shape) for v in (master, first_moment, second_moment)]
    held, picked = None, {}
    for which in (2, 0, 1):
        *held, picked[which] = adam_call(
            which, place_cur, place_next, got[which], states, held
        )
    weights = {k: exchange(picked[k]).reshape(slot_count * lines, LANES) for k in (0, 1, 2)}

    gate = project_call(quarters, weights[0], pieces, None)
    fwd_hidden = project_call(quarters, weights[1], pieces, gate)
    partial = down_call(weights[2], fwd_hidden)
    shares = lax.all_to_all(partial, "hid", split_axis=0, concat_axis=0, tiled=True)
    total = jnp.sum(shares.astype(F32), axis=0).astype(BF)
    returned = lax.all_to_all(
        total.reshape(slot_count, capacity, quarter), "slot", split_axis=0, concat_axis=0, tiled=True
    ).reshape(slot_count * capacity, quarter)
    out_rows = lax.dot_general(
        place_map, returned, (((0,), (0,)), ((), ())), preferred_element_type=F32
    ).astype(BF)
    return (out_rows, *[v.reshape(master.shape) for v in held])


def solution(mesh):
    shard = P(None, None, "hid", "slot")
    return jax.shard_map(
        shards,
        mesh=mesh,
        in_specs=(
            shard,
            shard,
            shard,
            P("slot", None, "hid", None),
            P("slot", None, None),
            P("slot", None, None),
            P("slot", None),
            P("slot", None),
            P(),
            P(),
            P("slot", "hid"),
            P("slot", None),
        ),
        out_specs=(P("slot", "hid"), shard, shard, shard),
        check_vma=False,
    )
```

```python
import functools

import jax
import jax.numpy as jnp
from jax import lax
from jax.experimental import pallas as pl
from jax.experimental.pallas import tpu as pltpu
from jax.sharding import PartitionSpec as P

desired_weight = 1.0
undesired_weight = 1.33
learn_rate = 0.004
decay_first = 0.9
decay_second = 0.999
correct_first = 0.9999734386011124
correct_second = 0.09520785288629043
adam_eps = 1e-08
weight_decay = 0.1

BF = jnp.bfloat16
F32 = jnp.float32
NT = (((1,), (1,)), ((), ()))
TN = (((0,), (0,)), ((), ()))
LANES = 128


def dot(a, b, dims=(((1,), (0,)), ((), ()))):
    return lax.dot_general(a, b, dims, preferred_element_type=F32)


def swap_map(first, second, tail=1):
    size = first * second * tail
    row = lax.broadcasted_iota(jnp.int32, (size, size), 0)
    col = lax.broadcasted_iota(jnp.int32, (size, size), 1)
    b, a, t = row // (first * tail), row // tail % first, row % tail
    return jnp.where(col == (a * second + b) * tail + t, 1.0, 0.0).astype(BF)


def whole(shape):
    return pl.BlockSpec(shape, lambda *_: (0,) * len(shape))


def limits(mib):
    return pltpu.CompilerParams(vmem_limit_bytes=mib << 20)


def scores_kernel(x_ref, r_ref, w_ref, a_ref, b_ref, h_ref, part_ref):
    units = h_ref.shape[0]
    both = dot(w_ref[0 : 2 * units], x_ref[...], NT)
    dh = dot(w_ref[2 * units :], r_ref[...], NT)
    gate, up = both[:units], both[units:]
    sigma = jax.nn.sigmoid(gate)
    hidden = (gate * sigma * up).astype(BF)
    h_ref[...] = hidden
    part_ref[...] = jnp.sum(hidden.astype(F32) * dh, axis=0, keepdims=True)
    a_ref[...] = dh * up * sigma * (1.0 + gate * (1.0 - sigma))
    b_ref[...] = dh * gate * sigma


def scores_call(inputs, direction, weights):
    rows, width = inputs.shape
    units = weights.shape[0] // 3
    block = 256
    tall = pl.BlockSpec((units, block), lambda i: (0, i))
    return pl.pallas_call(
        scores_kernel,
        grid=(rows // block,),
        in_specs=[
            pl.BlockSpec((block, width), lambda i: (i, 0)),
            pl.BlockSpec((block, width), lambda i: (i, 0)),
            pl.BlockSpec((3 * units, width), lambda i: (0, 0), pipeline_mode=pl.Buffered(1)),
        ],
        out_specs=[tall, tall, tall, pl.BlockSpec((1, block), lambda i: (0, i))],
        out_shape=[
            jax.ShapeDtypeStruct((units, rows), F32),
            jax.ShapeDtypeStruct((units, rows), F32),
            jax.ShapeDtypeStruct((units, rows), BF),
            jax.ShapeDtypeStruct((1, rows), F32),
        ],
        cost_estimate=pl.CostEstimate(
            flops=6 * rows * width * units, bytes_accessed=14 << 20, transcendentals=rows * units
        ),
        compiler_params=limits(32),
        name="scores",
    )(inputs, direction, weights)


def grads_kernel(sums_ref, sco_ref, lab_ref, a_ref, b_ref, h_ref, rows_ref, r_ref, x_ref, out_ref, lhs, held):
    step = pl.program_id(0)
    last = pl.num_programs(0) // 2 - 1
    units, rows = a_ref.shape
    wide = x_ref.shape[1]
    slots = out_ref.shape[0]

    @pl.when(step == 0)
    def _():
        center = jnp.sum(sums_ref[...][:, 0, 0:1]) / (slots * rows)
        q = jax.nn.sigmoid(sco_ref[...] - center)
        slope = q * (1.0 - q) * jnp.where(lab_ref[...] == 1, -desired_weight, undesired_weight)
        for k, term in enumerate((h_ref, a_ref, b_ref)):
            for i in range(rows // LANES):
                cols = slice(i * LANES, (i + 1) * LANES)
                lhs[k * units : (k + 1) * units, cols] = (
                    term[:, cols].astype(F32) * slope[i : i + 1]
                ).astype(BF)
        capacity = rows_ref.shape[0] // slots
        for s in range(slots):
            for j in range(rows_ref.shape[1] // LANES):
                out_ref[s, 288 + j * capacity : 288 + (j + 1) * capacity] = rows_ref[
                    s * capacity : (s + 1) * capacity, j * LANES : (j + 1) * LANES
                ]

    @pl.when(step <= last)
    def _():
        cols = pl.ds(pl.multiple_of(step * wide, wide), wide)
        held[0:units, cols] = dot(lhs[0:units], r_ref[...]).astype(BF)

    @pl.when(step > last)
    def _():
        cols = pl.ds(pl.multiple_of((step - last - 1) * wide, wide), wide)
        held[units:, cols] = dot(lhs[units:], x_ref[...]).astype(BF)

    def spread(k, line):
        swap = swap_map(16, 16)
        for pair in range(units // 32):
            halves = []
            for half in range(2):
                base = k * units + (2 * pair + half) * 16
                tiles = [held[base : base + 16, j * LANES : (j + 1) * LANES] for j in range(16)]
                halves.append(jnp.concatenate(tiles, axis=0))
            both = dot(swap, jnp.concatenate(halves, axis=1)).astype(BF)
            for half in range(2):
                for p in range(8):
                    at = (2 * pair + half) * 256 + p * 32
                    top = line + at % 96
                    out_ref[at // 96, top : top + 32] = both[
                        p * 32 : (p + 1) * 32, half * LANES : (half + 1) * LANES
                    ]

    @pl.when(step == last)
    def _():
        spread(0, 192)

    @pl.when(step == 2 * last + 1)
    def _():
        spread(1, 0)
        spread(2, 96)


def grads_call(sums, scores, labels, a, b, h, sent_rows, direction, inputs):
    units, rows = a.shape
    width = inputs.shape[1]
    slots = sums.shape[0]
    wide = 512
    steps = width // wide
    out = (slots, 288 + 64, LANES)
    return pl.pallas_call(
        grads_kernel,
        grid=(2 * steps,),
        in_specs=[whole(v.shape) for v in (sums, scores, labels, a, b, h, sent_rows)]
        + [
            pl.BlockSpec((rows, wide), lambda i: (0, jnp.minimum(i, steps - 1))),
            pl.BlockSpec((rows, wide), lambda i: (0, jnp.maximum(i - steps, 0))),
        ],
        out_specs=whole(out),
        out_shape=jax.ShapeDtypeStruct(out, BF),
        scratch_shapes=[pltpu.VMEM((3 * units, rows), BF), pltpu.VMEM((3 * units, width), BF)],
        cost_estimate=pl.CostEstimate(
            flops=6 * rows * width * units, bytes_accessed=12 << 20, transcendentals=rows
        ),
        compiler_params=limits(32),
        name="grads",
    )(sums, scores, labels, a, b, h, sent_rows, direction, inputs)


def adam_step(pc_ref, arr_ref, ms_ref, m1_ref, m2_ref, om_ref, o1_ref, o2_ref, total, fresh):
    total[...] = jnp.zeros_like(total)
    for s in range(arr_ref.shape[0]):
        total[pc_ref[s]] += arr_ref[s].astype(F32)
    for e in range(total.shape[0]):
        grad = total[e]
        master = ms_ref[e, 0]
        new_first = decay_first * m1_ref[e, 0] + (1.0 - decay_first) * grad
        new_second = decay_second * m2_ref[e, 0] + (1.0 - decay_second) * grad * grad
        update = new_first / correct_first / (jnp.sqrt(new_second / correct_second) + adam_eps)
        new_master = master - learn_rate * (update + weight_decay * master)
        om_ref[e, 0] = new_master
        o1_ref[e, 0] = new_first
        o2_ref[e, 0] = new_second
        fresh[e] = new_master.astype(BF)


def adam_pick_kernel(pc_ref, pn_ref, arr_ref, ms, m1, m2, om, o1, o2, pick_ref, total, fresh):
    adam_step(pc_ref, arr_ref, ms, m1, m2, om, o1, o2, total, fresh)
    for t in range(pick_ref.shape[0]):
        pick_ref[t] = fresh[pn_ref[t]]


def adam_split_kernel(pc_ref, arr_ref, ms, m1, m2, _a, _b, _c, om, o1, o2, piece_ref, total, fresh):
    adam_step(pc_ref, arr_ref, ms, m1, m2, om, o1, o2, total, fresh)
    experts = fresh.shape[0]
    turned = dot(swap_map(2, 4, 4), jnp.concatenate([fresh[e] for e in range(experts)], axis=1))
    for q in range(4):
        for e in range(experts):
            piece_ref[q, e] = turned[q * 8 : (q + 1) * 8, e * LANES : (e + 1) * LANES].astype(BF)


def adam_call(place_cur, place_next, arrived, states, held):
    slots = arrived.shape[0]
    experts, _, lines, _ = states[0].shape
    block = 32
    steps = lines // block
    first = 0 if held is None else 2
    state = pl.BlockSpec((experts, 1, block, LANES), lambda i: (0, first + i // steps, i % steps, 0))
    got = pl.BlockSpec((slots, block, LANES), lambda i: (0, first * steps + i, 0))
    smem = pl.BlockSpec(memory_space=pltpu.SMEM)
    shapes = [jax.ShapeDtypeStruct(s.shape, F32) for s in states]
    scratch = [pltpu.VMEM((experts, block, LANES), F32), pltpu.VMEM((experts, block, LANES), BF)]
    cost = pl.CostEstimate(flops=20 << 20, bytes_accessed=6 << 20, transcendentals=0)
    if held is None:
        return pl.pallas_call(
            adam_pick_kernel,
            grid=(2 * steps,),
            in_specs=[smem, smem, got, state, state, state],
            out_specs=[state, state, state, pl.BlockSpec((slots, block, LANES), lambda i: (0, i, 0))],
            out_shape=shapes + [jax.ShapeDtypeStruct((slots, 2 * lines, LANES), BF)],
            scratch_shapes=scratch,
            cost_estimate=cost,
            compiler_params=limits(24),
            name="adam_pick",
        )(place_cur, place_next, arrived, *states)
    return pl.pallas_call(
        adam_split_kernel,
        grid=(steps,),
        in_specs=[smem, got, state, state, state] + [pl.BlockSpec(memory_space=pl.ANY)] * 3,
        out_specs=[state, state, state, pl.BlockSpec((4, experts, 8, LANES), lambda i: (0, 0, i, 0))],
        out_shape=shapes + [jax.ShapeDtypeStruct((4, experts, 8 * steps, LANES), BF)],
        scratch_shapes=scratch,
        input_output_aliases={5: 0, 6: 1, 7: 2},
        cost_estimate=cost,
        compiler_params=limits(24),
        name="adam_split",
    )(place_cur, arrived, *states, *held)


def pick_kernel(pn_ref, p0, p1, p2, p3, out_ref):
    for t in range(out_ref.shape[0]):
        expert = pn_ref[t]
        own = [p[expert].astype(F32) for p in (p0, p1, p2, p3)]
        for a in range(3):
            out_ref[t, a * 32 : (a + 1) * 32] = jnp.concatenate(
                [v[a * 8 : (a + 1) * 8] for v in own], axis=0
            ).astype(BF)


def pick_call(place_next, pieces):
    slots = place_next.shape[0]
    shape = (slots, 4 * pieces[0].shape[1], LANES)
    return pl.pallas_call(
        pick_kernel,
        grid=(1,),
        in_specs=[pl.BlockSpec(memory_space=pltpu.SMEM)] + [whole(p.shape) for p in pieces],
        out_specs=whole(shape),
        out_shape=jax.ShapeDtypeStruct(shape, BF),
        cost_estimate=pl.CostEstimate(flops=1 << 20, bytes_accessed=2 << 20, transcendentals=0),
        compiler_params=limits(16),
        name="pick",
    )(place_next, *pieces)


def hidden_kernel(q_ref, w_ref, r0, r1, r2, r3, out_ref, mat):
    units = out_ref.shape[0]
    swap = swap_map(16, 16)
    for group in range(4):
        for a in range(3):
            both = jnp.concatenate(
                [
                    w_ref[group * 8 : group * 8 + 8, m * 96 + a * 32 : m * 96 + a * 32 + 32].reshape(
                        256, LANES
                    )
                    for m in range(2)
                ],
                axis=1,
            )
            turned = dot(swap, both).astype(BF)
            for m in range(2):
                top = m * units + (group * 3 + a) * 16
                for j in range(16):
                    mat[top : top + 16, j * LANES : (j + 1) * LANES] = turned[
                        j * 16 : (j + 1) * 16, m * LANES : (m + 1) * LANES
                    ]
    total = None
    for k, rows in enumerate((r0, r1, r2, r3)):
        quarter = rows.shape[1]
        start = pl.multiple_of(q_ref[k] * quarter, quarter)
        term = dot(mat[:, pl.ds(start, quarter)], rows[...], NT)
        total = term if total is None else total + term
    gate, up = total[:units], total[units:]
    out_ref[...] = (gate * jax.nn.sigmoid(gate) * up).astype(BF)


def hidden_call(quarters, packed, rows):
    units = packed.shape[0] * 6
    count, quarter = rows[0].shape
    return pl.pallas_call(
        hidden_kernel,
        grid=(1,),
        in_specs=[pl.BlockSpec(memory_space=pltpu.SMEM), whole(packed.shape)]
        + [whole(r.shape) for r in rows],
        out_specs=whole((units, count)),
        out_shape=jax.ShapeDtypeStruct((units, count), BF),
        scratch_shapes=[pltpu.VMEM((2 * units, 4 * quarter), BF)],
        cost_estimate=pl.CostEstimate(
            flops=16 * count * quarter * units, bytes_accessed=4 << 20, transcendentals=count * units
        ),
        compiler_params=limits(24),
        name="hidden",
    )(quarters, packed, *rows)


def unpack_kernel(w_ref, out_ref):
    swap = swap_map(16, 16)
    lines = w_ref.shape[1]
    row = lax.broadcasted_iota(jnp.int32, (256, 256), 0)
    col = lax.broadcasted_iota(jnp.int32, (256, 256), 1)
    k, j, s, b = row // 64, row // 16 % 4, row // 2 % 8, row % 2
    turn = jnp.where(col == ((s * 4 + k) * 2 + b) * 4 + j, 1.0, 0.0).astype(BF)
    for group in range(4):
        for a in range(lines // 32):
            turned = dot(
                turn, w_ref[group * 8 : group * 8 + 8, a * 32 : a * 32 + 32].reshape(256, LANES)
            ).astype(BF)
            top = (group * 3 + a) * 16
            for k in range(4):
                for j in range(4):
                    at = (k * 4 + j) * 16
                    out_ref[k, top : top + 16, j * LANES : (j + 1) * LANES] = turned[at : at + 16]


def unpack_call(packed):
    shape = (4, packed.shape[0] * 6, 4 * LANES)
    return pl.pallas_call(
        unpack_kernel,
        grid=(1,),
        in_specs=[whole(packed.shape)],
        out_specs=whole(shape),
        out_shape=jax.ShapeDtypeStruct(shape, BF),
        cost_estimate=pl.CostEstimate(flops=1 << 28, bytes_accessed=2 << 20, transcendentals=0),
        compiler_params=limits(16),
        name="unpack",
    )(packed)


def down_kernel(w_ref, h0, h1, h2, h3, out_ref):
    total = None
    for k, h in enumerate((h0, h1, h2, h3)):
        term = dot(h[...], w_ref[k], TN)
        total = term if total is None else total + term
    out_ref[...] = total.astype(BF)


def down_call(weights, hidden):
    units, count = hidden[0].shape
    quarter = weights.shape[2]
    return pl.pallas_call(
        down_kernel,
        grid=(1,),
        in_specs=[whole(weights.shape)] + [whole(h.shape) for h in hidden],
        out_specs=whole((count, quarter)),
        out_shape=jax.ShapeDtypeStruct((count, quarter), BF),
        cost_estimate=pl.CostEstimate(
            flops=8 * count * quarter * units, bytes_accessed=3 << 20, transcendentals=0
        ),
        compiler_params=limits(16),
        name="down",
    )(weights, *hidden)


def shards(
    master,
    first_moment,
    second_moment,
    slot_weights,
    back_rows,
    readout,
    ref_logratio,
    labels,
    place_cur,
    place_next,
    fwd_rows,
    routes,
):
    slot_count = lax.axis_size("slot")
    hid_count = lax.axis_size("hid")
    hid_index = lax.axis_index("hid").astype(jnp.int32)
    rows, width = back_rows.shape[1:]

    def pass_on(value, k):
        return lax.ppermute(value, "hid", [(i, (i + k) % hid_count) for i in range(hid_count)])

    def exchange(value):
        return lax.all_to_all(value, "slot", split_axis=0, concat_axis=0, tiled=True)

    capacity = 2 * fwd_rows.shape[0] // slot_count
    quarter = fwd_rows.shape[1]
    target = routes[:, 0]
    target_map = (target[:, None] == jnp.arange(slot_count, dtype=jnp.int32)[None, :]).astype(BF)
    order = jnp.arange(fwd_rows.shape[0], dtype=jnp.int32)
    below = (order[:, None] > order[None, :]).astype(BF)
    earlier = jnp.dot(below, target_map, preferred_element_type=F32)
    position = jnp.sum(earlier * target_map.astype(F32), axis=1).astype(jnp.int32)
    slot_place = target * capacity + position
    place_map = (
        slot_place[None, :] == jnp.arange(slot_count * capacity, dtype=jnp.int32)[:, None]
    ).astype(BF)
    sent_rows = jnp.dot(place_map, fwd_rows, preferred_element_type=F32).astype(BF)

    a, b, h, part = scores_call(back_rows[0], readout[0], slot_weights.reshape(-1, width))
    part = part.reshape(rows // LANES, LANES)
    policy = part
    for k in range(1, hid_count):
        policy = policy + pass_on(part, k)
    scores = policy - ref_logratio.reshape(part.shape)
    sums = exchange(jnp.broadcast_to(jnp.sum(scores), (slot_count, 1, LANES)))
    blocks = grads_call(
        sums, scores, labels.reshape(part.shape), a, b, h, sent_rows, readout[0], back_rows[0]
    )
    arrived = exchange(blocks)

    own_rows = arrived[:, 288:].reshape(slot_count, quarter // LANES, capacity, LANES)
    own_rows = own_rows.transpose(0, 2, 1, 3).reshape(slot_count * capacity, quarter)
    all_rows = [own_rows] + [pass_on(own_rows, k) for k in range(1, hid_count)]
    quarters = (hid_index + hid_count - jnp.arange(hid_count, dtype=jnp.int32)) % hid_count

    lines = 96
    shape = (master.shape[0], 3, lines, LANES)
    states = [v.reshape(shape) for v in (master, first_moment, second_moment)]
    *held, picked = adam_call(place_cur, place_next, arrived, states, None)
    gate_up = exchange(picked)
    *held, pieces = adam_call(place_cur, place_next, arrived, states, held)
    pieces = [
        lax.dynamic_index_in_dim(pieces, (hid_index + k) % hid_count, 0, keepdims=False)
        for k in range(hid_count)
    ]
    pieces = [pieces[0]] + [pass_on(pieces[k], k) for k in range(1, hid_count)]
    down = exchange(pick_call(place_next, pieces))

    hidden = hidden_call(quarters, gate_up, all_rows)
    hidden = [hidden] + [pass_on(hidden, k) for k in range(1, hid_count)]
    produced = down_call(unpack_call(down), hidden)
    returned = exchange(produced.reshape(slot_count, capacity, quarter))
    out_rows = lax.dot_general(
        place_map,
        returned.reshape(slot_count * capacity, quarter),
        (((0,), (0,)), ((), ())),
        preferred_element_type=F32,
    ).astype(BF)
    return (out_rows, *[v.reshape(master.shape) for v in held])


def solution(mesh):
    shard = P(None, None, "hid", "slot")
    return jax.shard_map(
        shards,
        mesh=mesh,
        in_specs=(
            shard,
            shard,
            shard,
            P("slot", None, "hid", None),
            P("slot", None, None),
            P("slot", None, None),
            P("slot", None),
            P("slot", None),
            P(),
            P(),
            P("slot", "hid"),
            P("slot", None),
        ),
        out_specs=(P("slot", "hid"), shard, shard, shard),
        check_vma=False,
    )
```

```python
import functools

import jax
import jax.numpy as jnp
from jax import lax
from jax.experimental import pallas as pl
from jax.experimental.pallas import tpu as pltpu
from jax.sharding import PartitionSpec as P

desired_weight = 1.0
undesired_weight = 1.33
learn_rate = 0.004
decay_first = 0.9
decay_second = 0.999
correct_first = 0.9999734386011124
correct_second = 0.09520785288629043
adam_eps = 1e-08
weight_decay = 0.1

BF = jnp.bfloat16
F32 = jnp.float32
NT = (((1,), (1,)), ((), ()))
TN = (((0,), (0,)), ((), ()))
LANES = 128
CAPACITY = 16
CHUNKS = 2
AHEAD = 3


def dot(a, b, dims=(((1,), (0,)), ((), ()))):
    return lax.dot_general(a, b, dims, preferred_element_type=F32)


def swap_map(first, second, tail=1):
    size = first * second * tail
    row = lax.broadcasted_iota(jnp.int32, (size, size), 0)
    col = lax.broadcasted_iota(jnp.int32, (size, size), 1)
    b, a, t = row // (first * tail), row // tail % first, row % tail
    return jnp.where(col == (a * second + b) * tail + t, 1.0, 0.0).astype(BF)


def piece_map():
    row = lax.broadcasted_iota(jnp.int32, (96, 96), 0)
    col = lax.broadcasted_iota(jnp.int32, (96, 96), 1)
    q, unit, j = row // 24, row // 4 % 6, row % 4
    return jnp.where(col == (unit * 4 + q) * 4 + j, 1.0, 0.0).astype(BF)


def whole(shape):
    return pl.BlockSpec(shape, lambda *_: (0,) * len(shape))


def single(shape):
    return pl.BlockSpec(shape, lambda *_: (0,) * len(shape), pipeline_mode=pl.Buffered(1))


def limits(mib):
    return pltpu.CompilerParams(vmem_limit_bytes=mib << 20)


def scores_kernel(
    own_ref, x_hbm, r_hbm, w_hbm, log_ref, route_ref, fwd_ref,
    x_ref, r_ref, a_ref, b_ref, h_ref, parts_ref, sent_ref, place_ref, w_ref, sems,
):
    rows = x_ref.shape[0]
    units = h_ref.shape[0]
    block = rows // CHUNKS
    pairs = [(w_hbm.at[pl.ds(0, 2 * units)], w_ref.at[pl.ds(0, 2 * units)])]
    for c in range(CHUNKS):
        part = pl.ds(c * block, block)
        pairs.append((x_hbm.at[part], x_ref.at[part]))
        if c == 0:
            down = pl.ds(2 * units, units)
            pairs.append((w_hbm.at[down], w_ref.at[down]))
        pairs.append((r_hbm.at[part], r_ref.at[part]))
    copies = [pltpu.make_async_copy(*pair, sems.at[k]) for k, pair in enumerate(pairs)]

    def arrive(k):
        copies[k].wait()
        if k + AHEAD < len(copies):
            copies[k + AHEAD].start()

    for copy in copies[:AHEAD]:
        copy.start()

    count = fwd_ref.shape[0]
    span = sent_ref.shape[0]
    slots = 2 * count // CAPACITY
    route = route_ref[...]
    named = route == lax.broadcasted_iota(jnp.int32, (slots, count), 0)
    before = lax.broadcasted_iota(jnp.int32, (count, count), 0) < lax.broadcasted_iota(
        jnp.int32, (count, count), 1
    )
    earlier = dot(jnp.where(named, 1.0, 0.0).astype(BF), jnp.where(before, 1.0, 0.0).astype(BF))
    position = jnp.sum(jnp.where(named, earlier, 0.0), axis=0, keepdims=True)
    place = route * CAPACITY + position.astype(jnp.int32)
    place_ref[...] = place
    hit = place == lax.broadcasted_iota(jnp.int32, (span, count), 0)
    sent_ref[...] = dot(jnp.where(hit, 1.0, 0.0).astype(BF), fwd_ref[...]).astype(BF)

    arrive(0)
    terms = []
    for c in range(CHUNKS):
        cols = slice(c * block, (c + 1) * block)
        arrive(2 * c + 1 + (c > 0))
        both = dot(w_ref[0 : 2 * units], x_ref[cols], NT)
        if c == 0:
            arrive(2)
        arrive(2 * c + 3)
        dh = dot(w_ref[2 * units :], r_ref[cols], NT)
        gate, up = both[:units], both[units:]
        sigma = jax.nn.sigmoid(gate)
        hidden = (gate * sigma * up).astype(BF)
        h_ref[:, cols] = hidden
        term = jnp.sum(hidden.astype(F32) * dh, axis=0, keepdims=True) - 0.25 * log_ref[:, cols]
        terms += [term[:, k * LANES : (k + 1) * LANES] for k in range(block // LANES)]
        a_ref[:, cols] = dh * up * sigma * (1.0 + gate * (1.0 - sigma))
        b_ref[:, cols] = dh * gate * sigma
    term = jnp.concatenate(terms, axis=0)
    for k in range(parts_ref.shape[0]):
        parts_ref[k] = term


def scores_call(own, inputs, direction, weights, ref_logratio, route, fwd_rows, everyone):
    rows, width = inputs.shape
    units = weights.shape[0] // 3
    span = 2 * fwd_rows.shape[0]
    hbm = pl.BlockSpec(memory_space=pltpu.HBM)
    vmem = pl.BlockSpec(memory_space=pltpu.VMEM)
    return pl.pallas_call(
        scores_kernel,
        in_specs=[pl.BlockSpec(memory_space=pltpu.SMEM), hbm, hbm, hbm, vmem, vmem, vmem],
        out_specs=[vmem] * 8,
        out_shape=[
            pltpu.VMEM((rows, width), BF),
            pltpu.VMEM((rows, width), BF),
            pltpu.VMEM((units, rows), F32),
            pltpu.VMEM((units, rows), F32),
            pltpu.VMEM((units, rows), BF),
            jax.ShapeDtypeStruct((everyone, rows // LANES, LANES), F32),
            pltpu.VMEM((span, fwd_rows.shape[1]), BF),
            jax.ShapeDtypeStruct((1, fwd_rows.shape[0]), jnp.int32),
        ],
        scratch_shapes=[
            pltpu.VMEM(weights.shape, BF),
            pltpu.SemaphoreType.DMA((2 * CHUNKS + 2,)),
        ],
        cost_estimate=pl.CostEstimate(
            flops=6 * rows * width * units, bytes_accessed=14 << 20, transcendentals=rows * units
        ),
        compiler_params=limits(48),
        name="scores",
    )(own, inputs, direction, weights, ref_logratio, route, fwd_rows)


def grads_kernel(own_ref, parts_ref, lab_ref, a_ref, b_ref, h_ref, sent_ref, r_ref, x_ref, out_ref, lhs, held):
    units, rows = a_ref.shape
    wide = 512
    slots = out_ref.shape[0]
    center = jnp.sum(parts_ref[...]) / (slots * rows)
    hids = parts_ref.shape[0] // slots
    q = jax.nn.sigmoid(jnp.sum(parts_ref[pl.ds(own_ref[0] * hids, hids)], axis=0) - center)
    slope = q * (1.0 - q) * jnp.where(lab_ref[...] == 1, -desired_weight, undesired_weight)
    for k, term in enumerate((a_ref, b_ref, h_ref)):
        for i in range(rows // LANES):
            cols = slice(i * LANES, (i + 1) * LANES)
            lhs[k * units : (k + 1) * units, cols] = (
                term[:, cols].astype(F32) * slope[i : i + 1]
            ).astype(BF)

    @pl.loop(0, x_ref.shape[1] // wide)
    def _(step):
        cols = pl.ds(pl.multiple_of(step * wide, wide), wide)
        held[0 : 2 * units, cols] = dot(lhs[0 : 2 * units], x_ref[:, cols]).astype(BF)
        held[2 * units :, cols] = dot(lhs[2 * units :], r_ref[:, cols]).astype(BF)

    swap = swap_map(16, 16)
    for k in range(3):
        for pair in range(units // 32):
            halves = []
            for half in range(2):
                base = k * units + (2 * pair + half) * 16
                tiles = [held[base : base + 16, j * LANES : (j + 1) * LANES] for j in range(16)]
                halves.append(jnp.concatenate(tiles, axis=0))
            both = dot(swap, jnp.concatenate(halves, axis=1)).astype(BF)
            for half in range(2):
                for p in range(8):
                    at = (2 * pair + half) * 256 + p * 32
                    top = k * 96 + at % 96
                    out_ref[at // 96, top : top + 32] = both[
                        p * 32 : (p + 1) * 32, half * LANES : (half + 1) * LANES
                    ]
    for s in range(slots):
        for j in range(sent_ref.shape[1] // LANES):
            top = 288 + j * CAPACITY
            out_ref[s, top : top + CAPACITY] = sent_ref[
                s * CAPACITY : (s + 1) * CAPACITY, j * LANES : (j + 1) * LANES
            ]


def grads_call(own, parts, labels, a, b, h, sent, direction, inputs, slots):
    units, rows = a.shape
    width = inputs.shape[1]
    vmem = pl.BlockSpec(memory_space=pltpu.VMEM)
    return pl.pallas_call(
        grads_kernel,
        in_specs=[pl.BlockSpec(memory_space=pltpu.SMEM)] + [vmem] * 8,
        out_specs=vmem,
        out_shape=jax.ShapeDtypeStruct((slots, 288 + 4 * CAPACITY, LANES), BF),
        scratch_shapes=[pltpu.VMEM((3 * units, rows), BF), pltpu.VMEM((3 * units, width), BF)],
        cost_estimate=pl.CostEstimate(
            flops=6 * rows * width * units, bytes_accessed=12 << 20, transcendentals=rows
        ),
        compiler_params=limits(24),
        name="grads",
    )(own, parts, labels, a, b, h, sent, direction, inputs)


def adam_step(pc_ref, arr_ref, ms_ref, m1_ref, m2_ref, total, fresh, outs=None):
    for sums in total:
        sums[...] = jnp.zeros_like(sums)
    for s in range(arr_ref.shape[0]):
        total[s % len(total)][pc_ref[s]] += arr_ref[s].astype(F32)
    for e in range(fresh.shape[0]):
        grad = functools.reduce(jnp.add, [sums[e] for sums in total])
        master = ms_ref[e, 0]
        new_first = decay_first * m1_ref[e, 0] + (1.0 - decay_first) * grad
        new_second = decay_second * m2_ref[e, 0] + (1.0 - decay_second) * grad * grad
        size = jnp.sqrt(new_second * (1.0 / correct_second)) + adam_eps
        update = new_first * (1.0 / correct_first) / size
        new_master = master - learn_rate * (update + weight_decay * master)
        if outs is not None:
            outs[0][e, 0] = new_master
            outs[1][e, 0] = new_first
            outs[2][e, 0] = new_second
        fresh[e] = new_master.astype(BF)


def adam_pick_kernel(info_ref, pc_ref, pn_ref, arr_ref, ms, m1, m2, pick_ref, p0, p1, p2, p3, t0, t1, fresh, turned):
    adam_step(pc_ref, arr_ref, ms, m1, m2, (t0, t1), fresh)
    step = pl.program_id(0)

    @pl.when(step < 2)
    def _():
        for t in range(pick_ref.shape[0]):
            pick_ref[t] = fresh[pn_ref[t]]

    @pl.when(step >= 2)
    def _():
        experts = fresh.shape[0]
        side = jnp.concatenate([fresh[e] for e in range(experts)], axis=1)
        turned[...] = dot(piece_map(), side).reshape(turned.shape)
        for k, piece_ref in enumerate((p0, p1, p2, p3)):
            mine = turned[info_ref[5 + k]]
            for e in range(experts):
                piece_ref[e] = mine[:, e * LANES : (e + 1) * LANES].astype(BF)


def adam_full_kernel(pc_ref, arr_ref, ms, m1, m2, om, o1, o2, t0, t1, fresh):
    adam_step(pc_ref, arr_ref, ms, m1, m2, (t0, t1), fresh, (om, o1, o2))


def adam_call(info, place_cur, place_next, arrived, states, full):
    slots = arrived.shape[0]
    experts, _, lines, _ = states[0].shape
    block = lines
    steps = lines // block
    smem = pl.BlockSpec(memory_space=pltpu.SMEM)
    state = pl.BlockSpec((experts, 1, block, LANES), lambda i: (0, i // steps, i % steps, 0))
    piece = pl.BlockSpec((slots, block, LANES), lambda i: (0, i, 0))
    scratch = [pltpu.VMEM((experts, block, LANES), t) for t in (F32, F32, BF)]
    cost = pl.CostEstimate(flops=20 << 20, bytes_accessed=6 << 20, transcendentals=0)
    if not full:
        return pl.pallas_call(
            adam_pick_kernel,
            grid=(3 * steps,),
            in_specs=[smem, smem, smem, piece, state, state, state],
            out_specs=[pl.BlockSpec((slots, block, LANES), lambda i: (0, jnp.minimum(i, 1), 0))]
            + [single((experts, lines // 4, LANES))] * 4,
            out_shape=[pltpu.HBM((slots, 2 * lines, LANES), BF)]
            + [jax.ShapeDtypeStruct((experts, lines // 4, LANES), BF)] * 4,
            scratch_shapes=scratch + [pltpu.VMEM((4, lines // 4, experts * LANES), F32)],
            cost_estimate=cost,
            compiler_params=limits(18),
            name="adam_pick",
        )(info, place_cur, place_next, arrived, *states)
    return pl.pallas_call(
        adam_full_kernel,
        grid=(3 * steps,),
        in_specs=[smem, piece, state, state, state],
        out_specs=[state, state, state],
        out_shape=[jax.ShapeDtypeStruct(s.shape, F32) for s in states],
        scratch_shapes=scratch,
        cost_estimate=cost,
        compiler_params=limits(60),
        name="adam_full",
    )(place_cur, arrived, *states)


def pick_kernel(pn_ref, p0, p1, p2, p3, out_ref):
    for t in range(out_ref.shape[0]):
        expert = pn_ref[t]
        own = [p[expert].astype(F32) for p in (p0, p1, p2, p3)]
        for a in range(3):
            out_ref[t, a * 32 : (a + 1) * 32] = jnp.concatenate(
                [v[a * 8 : (a + 1) * 8] for v in own], axis=0
            ).astype(BF)


def pick_call(place_next, pieces):
    slots = place_next.shape[0]
    shape = (slots, 4 * pieces[0].shape[1], LANES)
    return pl.pallas_call(
        pick_kernel,
        grid=(1,),
        in_specs=[pl.BlockSpec(memory_space=pltpu.SMEM)] + [whole(p.shape) for p in pieces],
        out_specs=whole(shape),
        out_shape=jax.ShapeDtypeStruct(shape, BF),
        cost_estimate=pl.CostEstimate(flops=1 << 20, bytes_accessed=2 << 20, transcendentals=0),
        compiler_params=limits(16),
        name="pick",
    )(place_next, *pieces)


def hidden_kernel(q_ref, w_ref, r0, r1, r2, r3, out_ref, mat):
    units = out_ref.shape[0]
    swap = swap_map(16, 16)
    for group in range(4):
        for a in range(3):
            both = jnp.concatenate(
                [
                    w_ref[group * 8 : group * 8 + 8, m * 96 + a * 32 : m * 96 + a * 32 + 32].reshape(
                        256, LANES
                    )
                    for m in range(2)
                ],
                axis=1,
            )
            turned = dot(swap, both).astype(BF)
            for m in range(2):
                top = m * units + (group * 3 + a) * 16
                for j in range(16):
                    mat[top : top + 16, j * LANES : (j + 1) * LANES] = turned[
                        j * 16 : (j + 1) * 16, m * LANES : (m + 1) * LANES
                    ]
    total = None
    for k, rows in enumerate((r0, r1, r2, r3)):
        quarter = rows.shape[1]
        start = pl.multiple_of(q_ref[1 + k] * quarter, quarter)
        term = dot(mat[:, pl.ds(start, quarter)], rows[...], NT)
        total = term if total is None else total + term
    gate, up = total[:units], total[units:]
    out_ref[...] = (gate * jax.nn.sigmoid(gate) * up).astype(BF)


def hidden_call(quarters, packed, rows):
    units = packed.shape[0] * 6
    count, quarter = rows[0].shape
    return pl.pallas_call(
        hidden_kernel,
        grid=(1,),
        in_specs=[pl.BlockSpec(memory_space=pltpu.SMEM), whole(packed.shape)]
        + [whole(r.shape) for r in rows],
        out_specs=whole((units, count)),
        out_shape=jax.ShapeDtypeStruct((units, count), BF),
        scratch_shapes=[pltpu.VMEM((2 * units, 4 * quarter), BF)],
        cost_estimate=pl.CostEstimate(
            flops=16 * count * quarter * units, bytes_accessed=4 << 20, transcendentals=count * units
        ),
        compiler_params=limits(24),
        name="hidden",
    )(quarters, packed, *rows)


def unpack_kernel(w_ref, out_ref):
    swap = swap_map(16, 16)
    lines = w_ref.shape[1]
    row = lax.broadcasted_iota(jnp.int32, (256, 256), 0)
    col = lax.broadcasted_iota(jnp.int32, (256, 256), 1)
    k, j, s, b = row // 64, row // 16 % 4, row // 2 % 8, row % 2
    turn = jnp.where(col == ((s * 4 + k) * 2 + b) * 4 + j, 1.0, 0.0).astype(BF)
    for group in range(4):
        for a in range(lines // 32):
            turned = dot(
                turn, w_ref[group * 8 : group * 8 + 8, a * 32 : a * 32 + 32].reshape(256, LANES)
            ).astype(BF)
            top = (group * 3 + a) * 16
            for k in range(4):
                for j in range(4):
                    at = (k * 4 + j) * 16
                    out_ref[k, top : top + 16, j * LANES : (j + 1) * LANES] = turned[at : at + 16]


def unpack_call(packed):
    shape = (4, packed.shape[0] * 6, 4 * LANES)
    return pl.pallas_call(
        unpack_kernel,
        grid=(1,),
        in_specs=[whole(packed.shape)],
        out_specs=whole(shape),
        out_shape=jax.ShapeDtypeStruct(shape, BF),
        cost_estimate=pl.CostEstimate(flops=1 << 28, bytes_accessed=2 << 20, transcendentals=0),
        compiler_params=limits(16),
        name="unpack",
    )(packed)


def down_kernel(w_ref, h0, h1, h2, h3, out_ref):
    total = None
    for k, h in enumerate((h0, h1, h2, h3)):
        term = dot(h[...], w_ref[k], TN)
        total = term if total is None else total + term
    out_ref[...] = total.astype(BF)


def down_call(weights, hidden):
    units, count = hidden[0].shape
    quarter = weights.shape[2]
    return pl.pallas_call(
        down_kernel,
        grid=(1,),
        in_specs=[whole(weights.shape)] + [whole(h.shape) for h in hidden],
        out_specs=whole((count, quarter)),
        out_shape=jax.ShapeDtypeStruct((count, quarter), BF),
        cost_estimate=pl.CostEstimate(
            flops=8 * count * quarter * units, bytes_accessed=3 << 20, transcendentals=0
        ),
        compiler_params=limits(16),
        name="down",
    )(weights, *hidden)


def shards(
    master,
    first_moment,
    second_moment,
    slot_weights,
    back_rows,
    readout,
    ref_logratio,
    labels,
    place_cur,
    place_next,
    fwd_rows,
    routes,
):
    slot_count = lax.axis_size("slot")
    hid_count = lax.axis_size("hid")
    hid_index = lax.axis_index("hid").astype(jnp.int32)
    _, width = back_rows.shape[1:]

    def pass_on(value, k):
        return lax.ppermute(value, "hid", [(i, (i + k) % hid_count) for i in range(hid_count)])

    def exchange(value):
        return lax.all_to_all(value, "slot", split_axis=0, concat_axis=0, tiled=True)

    capacity = CAPACITY
    quarter = fwd_rows.shape[1]
    everyone = slot_count * hid_count
    turns = jnp.arange(hid_count, dtype=jnp.int32)
    info = jnp.concatenate(
        [
            lax.axis_index("slot").astype(jnp.int32).reshape(1),
            (hid_index + hid_count - turns) % hid_count,
            (hid_index + turns) % hid_count,
        ]
    )
    inputs, direction, a, b, h, part, sent, slot_place = scores_call(
        info, back_rows[0], readout[0], slot_weights.reshape(-1, width), ref_logratio,
        routes.reshape(1, -1), fwd_rows, everyone,
    )
    parts = lax.all_to_all(part, ("slot", "hid"), split_axis=0, concat_axis=0, tiled=True)
    blocks = grads_call(
        info, parts, labels.reshape(part.shape[1:]), a, b, h, sent, direction, inputs, slot_count
    )
    arrived = exchange(blocks)

    lines = 96
    shape = (master.shape[0], 3, lines, LANES)
    states = [v.reshape(shape) for v in (master, first_moment, second_moment)]
    picked, *pieces = adam_call(info, place_cur, place_next, arrived, states, False)
    gate_up = exchange(picked)
    pieces = [pieces[0]] + [pass_on(pieces[k], k) for k in range(1, hid_count)]
    down = pick_call(place_next, pieces)
    down = exchange(down)

    own_rows = arrived[:, 3 * lines :].reshape(slot_count, quarter // LANES, capacity, LANES)
    own_rows = own_rows.transpose(0, 2, 1, 3).reshape(slot_count * capacity, quarter)
    all_rows = [own_rows] + [pass_on(own_rows, k) for k in range(1, hid_count)]
    held = adam_call(info, place_cur, place_next, arrived, states, True)

    hidden = hidden_call(info, gate_up, all_rows)
    hidden = [hidden] + [pass_on(hidden, k) for k in range(1, hid_count)]
    produced = down_call(unpack_call(down), hidden)
    returned = exchange(produced.reshape(slot_count, capacity, quarter))
    place_map = (
        slot_place == jnp.arange(slot_count * capacity, dtype=jnp.int32)[:, None]
    ).astype(BF)
    out_rows = lax.dot_general(
        place_map,
        returned.reshape(slot_count * capacity, quarter),
        (((0,), (0,)), ((), ())),
        preferred_element_type=F32,
    ).astype(BF)
    return (out_rows, *[v.reshape(master.shape) for v in held])


def solution(mesh):
    shard = P(None, None, "hid", "slot")
    return jax.shard_map(
        shards,
        mesh=mesh,
        in_specs=(
            shard,
            shard,
            shard,
            P("slot", None, "hid", None),
            P("slot", None, None),
            P("slot", None, None),
            P("slot", None),
            P("slot", None),
            P(),
            P(),
            P("slot", "hid"),
            P("slot", None),
        ),
        out_specs=(P("slot", "hid"), shard, shard, shard),
        check_vma=False,
    )
```

```python
import jax
import jax.numpy as jnp
from jax import lax
from jax.experimental import pallas as pl
from jax.experimental.pallas import tpu as pltpu
from jax.sharding import PartitionSpec as P

desired_weight = 1.0
undesired_weight = 1.33
learn_rate = 0.004
decay_first = 0.9
decay_second = 0.999
correct_first = 0.9999734386011124
correct_second = 0.09520785288629043
adam_eps = 1e-08
weight_decay = 0.1

BF = jnp.bfloat16
F32 = jnp.float32
NT = (((1,), (1,)), ((), ()))
TN = (((0,), (0,)), ((), ()))
LANES = 128
CAPACITY = 16
CHUNKS = 2
AHEAD = 3


def dot(a, b, dims=(((1,), (0,)), ((), ()))):
    return lax.dot_general(a, b, dims, preferred_element_type=F32)


def swap_map(first, second, tail=1):
    size = first * second * tail
    row = lax.broadcasted_iota(jnp.int32, (size, size), 0)
    col = lax.broadcasted_iota(jnp.int32, (size, size), 1)
    b, a, t = row // (first * tail), row // tail % first, row % tail
    return jnp.where(col == (a * second + b) * tail + t, 1.0, 0.0).astype(BF)


def piece_map():
    row = lax.broadcasted_iota(jnp.int32, (96, 96), 0)
    col = lax.broadcasted_iota(jnp.int32, (96, 96), 1)
    q, unit, j = row // 24, row // 4 % 6, row % 4
    return jnp.where(col == (unit * 4 + q) * 4 + j, 1.0, 0.0).astype(BF)


VM = pl.BlockSpec(memory_space=pltpu.VMEM)


def in_hbm(value):
    return pltpu.with_memory_space_constraint(value, pltpu.HBM)


def limits(mib):
    return pltpu.CompilerParams(vmem_limit_bytes=mib << 20)


def scores_kernel(
    x_hbm, r_hbm, w_hbm, log_ref, route_ref, fwd_ref,
    x_ref, r_ref, a_ref, b_ref, h_ref, parts_ref, sent_ref, place_ref, w_ref, sems,
):
    rows = x_ref.shape[0]
    units = h_ref.shape[0]
    block = rows // CHUNKS
    pairs = [(w_hbm.at[pl.ds(0, 2 * units)], w_ref.at[pl.ds(0, 2 * units)])]
    for c in range(CHUNKS):
        part = pl.ds(c * block, block)
        pairs.append((x_hbm.at[part], x_ref.at[part]))
        if c == 0:
            down = pl.ds(2 * units, units)
            pairs.append((w_hbm.at[down], w_ref.at[down]))
        pairs.append((r_hbm.at[part], r_ref.at[part]))
    copies = [pltpu.make_async_copy(*pair, sems.at[k]) for k, pair in enumerate(pairs)]

    def arrive(k):
        copies[k].wait()
        if k + AHEAD < len(copies):
            copies[k + AHEAD].start()

    for copy in copies[:AHEAD]:
        copy.start()

    count = fwd_ref.shape[0]
    span = sent_ref.shape[0]
    slots = 2 * count // CAPACITY
    route = route_ref[...]
    named = route == lax.broadcasted_iota(jnp.int32, (slots, count), 0)
    before = lax.broadcasted_iota(jnp.int32, (count, count), 0) < lax.broadcasted_iota(
        jnp.int32, (count, count), 1
    )
    earlier = dot(jnp.where(named, 1.0, 0.0).astype(BF), jnp.where(before, 1.0, 0.0).astype(BF))
    position = jnp.sum(jnp.where(named, earlier, 0.0), axis=0, keepdims=True)
    place = route * CAPACITY + position.astype(jnp.int32)
    place_ref[...] = place
    hit = place == lax.broadcasted_iota(jnp.int32, (span, count), 0)
    sent_ref[...] = dot(jnp.where(hit, 1.0, 0.0).astype(BF), fwd_ref[...]).astype(BF)

    arrive(0)
    terms = []
    for c in range(CHUNKS):
        cols = slice(c * block, (c + 1) * block)
        arrive(2 * c + 1 + (c > 0))
        both = dot(w_ref[0 : 2 * units], x_ref[cols], NT)
        if c == 0:
            arrive(2)
        arrive(2 * c + 3)
        dh = dot(w_ref[2 * units :], r_ref[cols], NT)
        gate, up = both[:units], both[units:]
        sigma = jax.nn.sigmoid(gate)
        hidden = (gate * sigma * up).astype(BF)
        h_ref[:, cols] = hidden
        term = jnp.sum(hidden.astype(F32) * dh, axis=0, keepdims=True) - 0.25 * log_ref[:, cols]
        terms += [term[:, k * LANES : (k + 1) * LANES] for k in range(block // LANES)]
        a_ref[:, cols] = dh * up * sigma * (1.0 + gate * (1.0 - sigma))
        b_ref[:, cols] = dh * gate * sigma
    term = jnp.concatenate(terms, axis=0)
    for k in range(parts_ref.shape[0]):
        parts_ref[k] = term


def scores_call(inputs, direction, weights, ref_logratio, route, fwd_rows, everyone):
    rows, width = inputs.shape
    units = weights.shape[0] // 3
    span = 2 * fwd_rows.shape[0]
    hbm = pl.BlockSpec(memory_space=pltpu.HBM)
    vmem = pl.BlockSpec(memory_space=pltpu.VMEM)
    return pl.pallas_call(
        scores_kernel,
        in_specs=[hbm, hbm, hbm, vmem, vmem, vmem],
        out_specs=[vmem] * 8,
        out_shape=[
            pltpu.VMEM((rows, width), BF),
            pltpu.VMEM((rows, width), BF),
            pltpu.VMEM((units, rows), F32),
            pltpu.VMEM((units, rows), F32),
            pltpu.VMEM((units, rows), BF),
            jax.ShapeDtypeStruct((everyone, rows // LANES, LANES), F32),
            pltpu.VMEM((span, fwd_rows.shape[1]), BF),
            jax.ShapeDtypeStruct((1, fwd_rows.shape[0]), jnp.int32),
        ],
        scratch_shapes=[
            pltpu.VMEM(weights.shape, BF),
            pltpu.SemaphoreType.DMA((2 * CHUNKS + 2,)),
        ],
        cost_estimate=pl.CostEstimate(
            flops=6 * rows * width * units, bytes_accessed=14 << 20, transcendentals=rows * units
        ),
        compiler_params=limits(48),
        name="scores",
    )(inputs, direction, weights, ref_logratio, route, fwd_rows)


def grads_kernel(parts_ref, lab_ref, a_ref, b_ref, h_ref, sent_ref, r_ref, x_ref, out_ref, lhs, held):
    units, rows = a_ref.shape
    wide = 512
    slots = out_ref.shape[0]
    center = jnp.sum(parts_ref[...]) / (slots * rows)
    hids = parts_ref.shape[0] // slots
    q = jax.nn.sigmoid(jnp.sum(parts_ref[pl.ds(lax.axis_index("slot") * hids, hids)], axis=0) - center)
    slope = q * (1.0 - q) * jnp.where(lab_ref[...] == 1, -desired_weight, undesired_weight)
    for k, term in enumerate((a_ref, b_ref, h_ref)):
        for i in range(rows // LANES):
            cols = slice(i * LANES, (i + 1) * LANES)
            lhs[k * units : (k + 1) * units, cols] = (
                term[:, cols].astype(F32) * slope[i : i + 1]
            ).astype(BF)

    @pl.loop(0, x_ref.shape[1] // wide)
    def _(step):
        cols = pl.ds(pl.multiple_of(step * wide, wide), wide)
        held[0 : 2 * units, cols] = dot(lhs[0 : 2 * units], x_ref[:, cols]).astype(BF)
        held[2 * units :, cols] = dot(lhs[2 * units :], r_ref[:, cols]).astype(BF)

    swap = swap_map(16, 16)
    for k in range(3):
        for pair in range(units // 32):
            halves = []
            for half in range(2):
                base = k * units + (2 * pair + half) * 16
                tiles = [held[base : base + 16, j * LANES : (j + 1) * LANES] for j in range(16)]
                halves.append(jnp.concatenate(tiles, axis=0))
            both = dot(swap, jnp.concatenate(halves, axis=1)).astype(BF)
            for half in range(2):
                for p in range(8):
                    at = (2 * pair + half) * 256 + p * 32
                    top = k * 96 + at % 96
                    out_ref[at // 96, top : top + 32] = both[
                        p * 32 : (p + 1) * 32, half * LANES : (half + 1) * LANES
                    ]
    for s in range(slots):
        for j in range(sent_ref.shape[1] // LANES):
            top = 288 + j * CAPACITY
            out_ref[s, top : top + CAPACITY] = sent_ref[
                s * CAPACITY : (s + 1) * CAPACITY, j * LANES : (j + 1) * LANES
            ]


def grads_call(parts, labels, a, b, h, sent, direction, inputs, slots):
    units, rows = a.shape
    width = inputs.shape[1]
    vmem = pl.BlockSpec(memory_space=pltpu.VMEM)
    return pl.pallas_call(
        grads_kernel,
        in_specs=[vmem] * 8,
        out_specs=vmem,
        out_shape=jax.ShapeDtypeStruct((slots, 288 + 4 * CAPACITY, LANES), BF),
        scratch_shapes=[pltpu.VMEM((3 * units, rows), BF), pltpu.VMEM((3 * units, width), BF)],
        cost_estimate=pl.CostEstimate(
            flops=6 * rows * width * units, bytes_accessed=12 << 20, transcendentals=rows
        ),
        compiler_params=limits(6),
        name="grads",
    )(parts, labels, a, b, h, sent, direction, inputs)


def adam_update(master, first, second, grad):
    new_first = decay_first * first + (1.0 - decay_first) * grad
    new_second = decay_second * second + (1.0 - decay_second) * grad * grad
    size = jnp.sqrt(new_second * (1.0 / correct_second)) + adam_eps
    update = new_first * (1.0 / correct_first) / size
    return master - learn_rate * (update + weight_decay * master), new_first, new_second


def updated_master(master, first, second, grad):
    step = (learn_rate * decay_first / correct_first) * first + (
        learn_rate * (1.0 - decay_first) / correct_first
    ) * grad
    second = (decay_second / correct_second) * second + (
        (1.0 - decay_second) / correct_second
    ) * (grad * grad)
    size = second * lax.rsqrt(second) + adam_eps
    return (1.0 - learn_rate * weight_decay) * master - step / size


def sum_experts(pc_ref, arr_ref, sums):
    lines = sums[0].shape[1]
    for part in sums:
        part[...] = jnp.zeros_like(part)
    for s in range(arr_ref.shape[0]):
        sums[s % len(sums)][pc_ref[s]] += arr_ref[s, 0:lines].astype(F32)


def adam_pick_kernel(
    pc_ref, pn_ref, arr_ref, ms, m1, m2,
    pick_hbm, p0, p1, p2, p3, rows_hbm, s0, s1, fresh, turned, picks, split, rows, sems,
):
    slots = arr_ref.shape[0]
    experts, _, lines, _ = ms.shape
    for s in range(slots):
        for j in range(rows.shape[1] // LANES):
            top = 3 * lines + j * CAPACITY
            rows[s * CAPACITY : (s + 1) * CAPACITY, j * LANES : (j + 1) * LANES] = arr_ref[
                s, top : top + CAPACITY
            ]
    writes = [pltpu.make_async_copy(rows, rows_hbm, sems.at[6])]
    writes[0].start()
    sum_experts(pc_ref, arr_ref, (s0, s1))
    for which in range(3):
        part = slice(which * lines, (which + 1) * lines)
        for e in range(experts):
            at = (e, which)
            grad = s0[e, part] + s1[e, part]
            fresh[e] = updated_master(ms[at], m1[at], m2[at], grad).astype(BF)
        if which < 2:
            for t in range(slots):
                picks[which, t] = fresh[pn_ref[t]]
            part = pick_hbm.at[:, pl.ds(which * lines, lines)]
            writes.append(pltpu.make_async_copy(picks.at[which], part, sems.at[which]))
            writes[-1].start()
    side = jnp.concatenate([fresh[e] for e in range(experts)], axis=1)
    turned[...] = dot(piece_map(), side).reshape(turned.shape)
    hid = lax.axis_index("hid")
    for k, piece_ref in enumerate((p0, p1, p2, p3)):
        mine = turned[lax.rem(hid + k, 4)]
        for e in range(experts):
            split[k, e] = mine[:, e * LANES : (e + 1) * LANES].astype(BF)
        writes.append(pltpu.make_async_copy(split.at[k], piece_ref, sems.at[2 + k]))
        writes[-1].start()
    for write in writes:
        write.wait()


def adam_pick_call(place_cur, place_next, arrived, states):
    slots = arrived.shape[0]
    experts, _, lines, _ = states[0].shape
    smem = pl.BlockSpec(memory_space=pltpu.SMEM)
    vmem = pl.BlockSpec(memory_space=pltpu.VMEM)
    rows_shape = (slots * CAPACITY, (arrived.shape[1] - 3 * lines) // CAPACITY * LANES)
    return pl.pallas_call(
        adam_pick_kernel,
        in_specs=[smem, smem] + [vmem] * 4,
        out_specs=[pl.BlockSpec(memory_space=pltpu.HBM)] * 6,
        out_shape=[pltpu.HBM((slots, 2 * lines, LANES), BF)]
        + [pltpu.HBM((experts, lines // 4, LANES), BF)] * 4
        + [pltpu.HBM(rows_shape, BF)],
        scratch_shapes=[pltpu.VMEM((experts, 3 * lines, LANES), F32)] * 2
        + [
            pltpu.VMEM((experts, lines, LANES), BF),
            pltpu.VMEM((4, lines // 4, experts * LANES), F32),
            pltpu.VMEM((2, slots, lines, LANES), BF),
            pltpu.VMEM((4, experts, lines // 4, LANES), BF),
            pltpu.VMEM(rows_shape, BF),
            pltpu.SemaphoreType.DMA((7,)),
        ],
        cost_estimate=pl.CostEstimate(flops=20 << 20, bytes_accessed=6 << 20, transcendentals=0),
        compiler_params=limits(10),
        name="adam_pick",
    )(place_cur, place_next, arrived, *states)


def adam_full_kernel(pc_ref, arr_ref, ms, m1, m2, om, o1, o2, s0, s1):
    sum_experts(pc_ref, arr_ref, (s0, s1))
    for e in range(ms.shape[0]):
        om[e, 0], o1[e, 0], o2[e, 0] = adam_update(ms[e, 0], m1[e, 0], m2[e, 0], s0[e] + s1[e])


def adam_full_call(place_cur, arrived, states):
    slots = arrived.shape[0]
    experts, count, lines, _ = states[0].shape
    state = pl.BlockSpec((experts, 1, lines, LANES), lambda i: (0, i, 0, 0))
    return pl.pallas_call(
        adam_full_kernel,
        grid=(count,),
        in_specs=[
            pl.BlockSpec(memory_space=pltpu.SMEM),
            pl.BlockSpec((slots, lines, LANES), lambda i: (0, i, 0)),
            state, state, state,
        ],
        out_specs=[state, state, state],
        out_shape=[jax.ShapeDtypeStruct(s.shape, F32) for s in states],
        scratch_shapes=[pltpu.VMEM((experts, lines, LANES), F32)] * 2,
        cost_estimate=pl.CostEstimate(flops=20 << 20, bytes_accessed=6 << 20, transcendentals=0),
        compiler_params=limits(60),
        name="adam_full",
    )(place_cur, arrived, *states)


def pick_kernel(pn_ref, p0, p1, p2, p3, out_ref):
    for t in range(out_ref.shape[0]):
        expert = pn_ref[t]
        own = [p[expert].astype(F32) for p in (p0, p1, p2, p3)]
        for a in range(3):
            out_ref[t, a * 32 : (a + 1) * 32] = jnp.concatenate(
                [v[a * 8 : (a + 1) * 8] for v in own], axis=0
            ).astype(BF)


def pick_call(place_next, pieces):
    slots = place_next.shape[0]
    shape = (slots, 4 * pieces[0].shape[1], LANES)
    return pl.pallas_call(
        pick_kernel,
        in_specs=[pl.BlockSpec(memory_space=pltpu.SMEM)] + [VM] * len(pieces),
        out_specs=VM,
        out_shape=jax.ShapeDtypeStruct(shape, BF),
        cost_estimate=pl.CostEstimate(flops=1 << 20, bytes_accessed=2 << 20, transcendentals=0),
        compiler_params=limits(4),
        name="pick",
    )(place_next, *pieces)


def hidden_kernel(w_ref, r0, r1, r2, r3, out_ref, mat):
    units = out_ref.shape[0]
    swap = swap_map(16, 16)
    for group in range(4):
        for a in range(3):
            both = jnp.concatenate(
                [
                    w_ref[group * 8 : group * 8 + 8, m * 96 + a * 32 : m * 96 + a * 32 + 32].reshape(
                        256, LANES
                    )
                    for m in range(2)
                ],
                axis=1,
            )
            turned = dot(swap, both).astype(BF)
            for m in range(2):
                top = m * units + (group * 3 + a) * 16
                for j in range(16):
                    mat[top : top + 16, j * LANES : (j + 1) * LANES] = turned[
                        j * 16 : (j + 1) * 16, m * LANES : (m + 1) * LANES
                    ]
    total = None
    for k, rows in enumerate((r0, r1, r2, r3)):
        quarter = rows.shape[1]
        turn = lax.rem(lax.axis_index("hid") + 4 - k, 4)
        start = pl.multiple_of(turn * quarter, quarter)
        term = dot(mat[:, pl.ds(start, quarter)], rows[...], NT)
        total = term if total is None else total + term
    gate, up = total[:units], total[units:]
    out_ref[...] = (gate * jax.nn.sigmoid(gate) * up).astype(BF)


def hidden_call(packed, rows):
    units = packed.shape[0] * 6
    count, quarter = rows[0].shape
    return pl.pallas_call(
        hidden_kernel,
        in_specs=[VM] * (1 + len(rows)),
        out_specs=VM,
        out_shape=jax.ShapeDtypeStruct((units, count), BF),
        scratch_shapes=[pltpu.VMEM((2 * units, 4 * quarter), BF)],
        cost_estimate=pl.CostEstimate(
            flops=16 * count * quarter * units, bytes_accessed=4 << 20, transcendentals=count * units
        ),
        compiler_params=limits(6),
        name="hidden",
    )(packed, *rows)


def unpack_kernel(w_ref, out_ref):
    swap = swap_map(16, 16)
    lines = w_ref.shape[1]
    row = lax.broadcasted_iota(jnp.int32, (256, 256), 0)
    col = lax.broadcasted_iota(jnp.int32, (256, 256), 1)
    k, j, s, b = row // 64, row // 16 % 4, row // 2 % 8, row % 2
    turn = jnp.where(col == ((s * 4 + k) * 2 + b) * 4 + j, 1.0, 0.0).astype(BF)
    for group in range(4):
        for a in range(lines // 32):
            turned = dot(
                turn, w_ref[group * 8 : group * 8 + 8, a * 32 : a * 32 + 32].reshape(256, LANES)
            ).astype(BF)
            top = (group * 3 + a) * 16
            for k in range(4):
                for j in range(4):
                    at = (k * 4 + j) * 16
                    out_ref[k, top : top + 16, j * LANES : (j + 1) * LANES] = turned[at : at + 16]


def unpack_call(packed):
    shape = (4, packed.shape[0] * 6, 4 * LANES)
    return pl.pallas_call(
        unpack_kernel,
        in_specs=[VM],
        out_specs=VM,
        out_shape=jax.ShapeDtypeStruct(shape, BF),
        cost_estimate=pl.CostEstimate(flops=1 << 28, bytes_accessed=2 << 20, transcendentals=0),
        compiler_params=limits(4),
        name="unpack",
    )(packed)


def down_kernel(w_ref, h0, h1, h2, h3, out_ref):
    total = None
    for k, h in enumerate((h0, h1, h2, h3)):
        term = dot(h[...], w_ref[k], TN)
        total = term if total is None else total + term
    out_ref[...] = total.astype(BF)


def down_call(weights, hidden):
    units, count = hidden[0].shape
    quarter = weights.shape[2]
    return pl.pallas_call(
        down_kernel,
        in_specs=[VM] * (1 + len(hidden)),
        out_specs=VM,
        out_shape=jax.ShapeDtypeStruct((count, quarter), BF),
        cost_estimate=pl.CostEstimate(
            flops=8 * count * quarter * units, bytes_accessed=3 << 20, transcendentals=0
        ),
        compiler_params=limits(4),
        name="down",
    )(weights, *hidden)


def shards(
    master,
    first_moment,
    second_moment,
    slot_weights,
    back_rows,
    readout,
    ref_logratio,
    labels,
    place_cur,
    place_next,
    fwd_rows,
    routes,
):
    slot_count = lax.axis_size("slot")
    hid_count = lax.axis_size("hid")
    _, width = back_rows.shape[1:]

    def pass_on(value, k):
        return lax.ppermute(value, "hid", [(i, (i + k) % hid_count) for i in range(hid_count)])

    def exchange(value):
        return lax.all_to_all(value, "slot", split_axis=0, concat_axis=0, tiled=True)

    capacity = CAPACITY
    quarter = fwd_rows.shape[1]
    everyone = slot_count * hid_count
    inputs, direction, a, b, h, part, sent, slot_place = scores_call(
        back_rows[0], readout[0], slot_weights.reshape(-1, width), ref_logratio,
        routes.reshape(1, -1), fwd_rows, everyone,
    )
    parts = lax.all_to_all(part, ("slot", "hid"), split_axis=0, concat_axis=0, tiled=True)
    blocks = grads_call(
        parts, labels.reshape(part.shape[1:]), a, b, h, sent, direction, inputs, slot_count
    )
    arrived = exchange(blocks)

    lines = 96
    shape = (master.shape[0], 3, lines, LANES)
    states = [v.reshape(shape) for v in (master, first_moment, second_moment)]
    picked, *pieces, own_rows = adam_pick_call(place_cur, place_next, arrived, states)
    far_rows = pass_on(own_rows, 2)
    all_rows = [own_rows, pass_on(own_rows, 1), far_rows, pass_on(own_rows, 3)]

    gate_up = in_hbm(exchange(picked))
    pieces = [pieces[0]] + [pass_on(pieces[k], k) for k in range(1, hid_count)]
    down = pick_call(place_next, pieces)
    down = exchange(down)

    held = adam_full_call(place_cur, arrived, states)

    hidden = hidden_call(gate_up, all_rows)
    hidden = [hidden] + [pass_on(hidden, k) for k in range(1, hid_count)]
    produced = down_call(unpack_call(down), hidden)
    returned = exchange(produced.reshape(slot_count, capacity, quarter))
    place_map = (
        slot_place == jnp.arange(slot_count * capacity, dtype=jnp.int32)[:, None]
    ).astype(BF)
    out_rows = lax.dot_general(
        place_map,
        returned.reshape(slot_count * capacity, quarter),
        (((0,), (0,)), ((), ())),
        preferred_element_type=F32,
    ).astype(BF)
    return (out_rows, *[v.reshape(master.shape) for v in held])


def solution(mesh):
    shard = P(None, None, "hid", "slot")
    return jax.shard_map(
        shards,
        mesh=mesh,
        in_specs=(
            shard,
            shard,
            shard,
            P("slot", None, "hid", None),
            P("slot", None, None),
            P("slot", None, None),
            P("slot", None),
            P("slot", None),
            P(),
            P(),
            P("slot", "hid"),
            P("slot", None),
        ),
        out_specs=(P("slot", "hid"), shard, shard, shard),
        check_vma=False,
    )
```

```python
import jax
import jax.numpy as jnp
from jax import lax
from jax.experimental import pallas as pl
from jax.experimental.pallas import tpu as pltpu
from jax.sharding import PartitionSpec as P

desired_weight = 1.0
undesired_weight = 1.33
learn_rate = 0.004
decay_first = 0.9
decay_second = 0.999
correct_first = 0.9999734386011124
correct_second = 0.09520785288629043
adam_eps = 1e-08
weight_decay = 0.1

BF = jnp.bfloat16
F32 = jnp.float32
NT = (((1,), (1,)), ((), ()))
TN = (((0,), (0,)), ((), ()))
LANES = 128
CAPACITY = 16
CHUNKS = 2
AHEAD = 3


def dot(a, b, dims=(((1,), (0,)), ((), ()))):
    return lax.dot_general(a, b, dims, preferred_element_type=F32)


def swap_map(first, second, tail=1):
    size = first * second * tail
    row = lax.broadcasted_iota(jnp.int32, (size, size), 0)
    col = lax.broadcasted_iota(jnp.int32, (size, size), 1)
    b, a, t = row // (first * tail), row // tail % first, row % tail
    return jnp.where(col == (a * second + b) * tail + t, 1.0, 0.0).astype(BF)


def piece_map():
    row = lax.broadcasted_iota(jnp.int32, (96, 96), 0)
    col = lax.broadcasted_iota(jnp.int32, (96, 96), 1)
    q, unit, j = row // 24, row // 4 % 6, row % 4
    return jnp.where(col == (unit * 4 + q) * 4 + j, 1.0, 0.0).astype(BF)


VM = pl.BlockSpec(memory_space=pltpu.VMEM)


def in_hbm(value):
    return pltpu.with_memory_space_constraint(value, pltpu.HBM)


def limits(mib):
    return pltpu.CompilerParams(vmem_limit_bytes=mib << 20)


def scores_kernel(
    x_hbm, r_hbm, w_hbm, log_ref, route_ref, fwd_ref,
    x_ref, r_ref, a_ref, b_ref, h_ref, parts_ref, sent_ref, place_ref, w_ref, sems,
):
    rows = x_ref.shape[0]
    units = h_ref.shape[0]
    block = rows // CHUNKS
    pairs = [(w_hbm.at[pl.ds(0, 2 * units)], w_ref.at[pl.ds(0, 2 * units)])]
    for c in range(CHUNKS):
        part = pl.ds(c * block, block)
        pairs.append((x_hbm.at[part], x_ref.at[part]))
        if c == 0:
            down = pl.ds(2 * units, units)
            pairs.append((w_hbm.at[down], w_ref.at[down]))
        pairs.append((r_hbm.at[part], r_ref.at[part]))
    copies = [pltpu.make_async_copy(*pair, sems.at[k]) for k, pair in enumerate(pairs)]

    def arrive(k):
        copies[k].wait()
        if k + AHEAD < len(copies):
            copies[k + AHEAD].start()

    for copy in copies[:AHEAD]:
        copy.start()

    count = fwd_ref.shape[0]
    span = sent_ref.shape[0]
    slots = 2 * count // CAPACITY
    route = route_ref[...]
    named = route == lax.broadcasted_iota(jnp.int32, (slots, count), 0)
    before = lax.broadcasted_iota(jnp.int32, (count, count), 0) < lax.broadcasted_iota(
        jnp.int32, (count, count), 1
    )
    earlier = dot(jnp.where(named, 1.0, 0.0).astype(BF), jnp.where(before, 1.0, 0.0).astype(BF))
    position = jnp.sum(jnp.where(named, earlier, 0.0), axis=0, keepdims=True)
    place = route * CAPACITY + position.astype(jnp.int32)
    place_ref[...] = place
    hit = place == lax.broadcasted_iota(jnp.int32, (span, count), 0)
    sent_ref[...] = dot(jnp.where(hit, 1.0, 0.0).astype(BF), fwd_ref[...]).astype(BF)

    arrive(0)
    terms = []
    for c in range(CHUNKS):
        cols = slice(c * block, (c + 1) * block)
        arrive(2 * c + 1 + (c > 0))
        both = dot(w_ref[0 : 2 * units], x_ref[cols], NT)
        if c == 0:
            arrive(2)
        arrive(2 * c + 3)
        dh = dot(w_ref[2 * units :], r_ref[cols], NT)
        gate, up = both[:units], both[units:]
        sigma = jax.nn.sigmoid(gate)
        hidden = (gate * sigma * up).astype(BF)
        h_ref[:, cols] = hidden
        term = jnp.sum(hidden.astype(F32) * dh, axis=0, keepdims=True) - 0.25 * log_ref[:, cols]
        terms += [term[:, k * LANES : (k + 1) * LANES] for k in range(block // LANES)]
        a_ref[:, cols] = dh * up * sigma * (1.0 + gate * (1.0 - sigma))
        b_ref[:, cols] = dh * gate * sigma
    term = jnp.concatenate(terms, axis=0)
    for k in range(parts_ref.shape[0]):
        parts_ref[k] = term


def scores_call(inputs, direction, weights, ref_logratio, route, fwd_rows, everyone):
    rows, width = inputs.shape
    units = weights.shape[0] // 3
    span = 2 * fwd_rows.shape[0]
    hbm = pl.BlockSpec(memory_space=pltpu.HBM)
    vmem = pl.BlockSpec(memory_space=pltpu.VMEM)
    return pl.pallas_call(
        scores_kernel,
        in_specs=[hbm, hbm, hbm, vmem, vmem, vmem],
        out_specs=[vmem] * 8,
        out_shape=[
            pltpu.VMEM((rows, width), BF),
            pltpu.VMEM((rows, width), BF),
            pltpu.VMEM((units, rows), F32),
            pltpu.VMEM((units, rows), F32),
            pltpu.VMEM((units, rows), BF),
            jax.ShapeDtypeStruct((everyone, rows // LANES, LANES), F32),
            pltpu.VMEM((span, fwd_rows.shape[1]), BF),
            jax.ShapeDtypeStruct((1, fwd_rows.shape[0]), jnp.int32),
        ],
        scratch_shapes=[
            pltpu.VMEM(weights.shape, BF),
            pltpu.SemaphoreType.DMA((2 * CHUNKS + 2,)),
        ],
        cost_estimate=pl.CostEstimate(
            flops=6 * rows * width * units, bytes_accessed=14 << 20, transcendentals=rows * units
        ),
        compiler_params=limits(48),
        name="scores",
    )(inputs, direction, weights, ref_logratio, route, fwd_rows)


def grads_kernel(parts_ref, lab_ref, a_ref, b_ref, h_ref, sent_ref, r_ref, x_ref, out_ref, lhs, held):
    units, rows = a_ref.shape
    wide = 512
    slots = out_ref.shape[0]
    center = jnp.sum(parts_ref[...]) / (slots * rows)
    hids = parts_ref.shape[0] // slots
    q = jax.nn.sigmoid(jnp.sum(parts_ref[pl.ds(lax.axis_index("slot") * hids, hids)], axis=0) - center)
    slope = q * (1.0 - q) * jnp.where(lab_ref[...] == 1, -desired_weight, undesired_weight)
    for k, term in enumerate((a_ref, b_ref, h_ref)):
        for i in range(rows // LANES):
            cols = slice(i * LANES, (i + 1) * LANES)
            lhs[k * units : (k + 1) * units, cols] = (
                term[:, cols].astype(F32) * slope[i : i + 1]
            ).astype(BF)

    @pl.loop(0, x_ref.shape[1] // wide)
    def _(step):
        cols = pl.ds(pl.multiple_of(step * wide, wide), wide)
        held[0 : 2 * units, cols] = dot(lhs[0 : 2 * units], x_ref[:, cols]).astype(BF)
        held[2 * units :, cols] = dot(lhs[2 * units :], r_ref[:, cols]).astype(BF)

    swap = swap_map(16, 16)
    for k in range(3):
        for pair in range(units // 32):
            halves = []
            for half in range(2):
                base = k * units + (2 * pair + half) * 16
                tiles = [held[base : base + 16, j * LANES : (j + 1) * LANES] for j in range(16)]
                halves.append(jnp.concatenate(tiles, axis=0))
            both = dot(swap, jnp.concatenate(halves, axis=1)).astype(BF)
            for half in range(2):
                for p in range(8):
                    at = (2 * pair + half) * 256 + p * 32
                    top = k * 96 + at % 96
                    out_ref[at // 96, top : top + 32] = both[
                        p * 32 : (p + 1) * 32, half * LANES : (half + 1) * LANES
                    ]
    for s in range(slots):
        for j in range(sent_ref.shape[1] // LANES):
            top = 288 + j * CAPACITY
            out_ref[s, top : top + CAPACITY] = sent_ref[
                s * CAPACITY : (s + 1) * CAPACITY, j * LANES : (j + 1) * LANES
            ]


def grads_call(parts, labels, a, b, h, sent, direction, inputs, slots):
    units, rows = a.shape
    width = inputs.shape[1]
    vmem = pl.BlockSpec(memory_space=pltpu.VMEM)
    return pl.pallas_call(
        grads_kernel,
        in_specs=[vmem] * 8,
        out_specs=vmem,
        out_shape=jax.ShapeDtypeStruct((slots, 288 + 4 * CAPACITY, LANES), BF),
        scratch_shapes=[pltpu.VMEM((3 * units, rows), BF), pltpu.VMEM((3 * units, width), BF)],
        cost_estimate=pl.CostEstimate(
            flops=6 * rows * width * units, bytes_accessed=12 << 20, transcendentals=rows
        ),
        compiler_params=limits(6),
        name="grads",
    )(parts, labels, a, b, h, sent, direction, inputs)


def adam_update(master, first, second, grad):
    new_first = decay_first * first + (1.0 - decay_first) * grad
    new_second = decay_second * second + (1.0 - decay_second) * grad * grad
    size = jnp.sqrt(new_second * (1.0 / correct_second)) + adam_eps
    update = new_first * (1.0 / correct_first) / size
    return master - learn_rate * (update + weight_decay * master), new_first, new_second


def updated_master(master, first, second, grad):
    step = (learn_rate * decay_first / correct_first) * first + (
        learn_rate * (1.0 - decay_first) / correct_first
    ) * grad
    second = (decay_second / correct_second) * second + (
        (1.0 - decay_second) / correct_second
    ) * (grad * grad)
    size = second * lax.rsqrt(second) + adam_eps
    return (1.0 - learn_rate * weight_decay) * master - step / size


def sum_experts(pc_ref, arr_ref, sums):
    lines = sums[0].shape[1]
    for part in sums:
        part[...] = jnp.zeros_like(part)
    for s in range(arr_ref.shape[0]):
        sums[s % len(sums)][pc_ref[s]] += arr_ref[s, 0:lines].astype(F32)


def adam_pick_kernel(
    pc_ref, pn_ref, arr_ref, ms, m1, m2,
    pick_hbm, p0, p1, p2, p3, rows_hbm, s0, s1, fresh, turned, picks, split, rows, sems,
):
    slots = arr_ref.shape[0]
    experts, _, lines, _ = ms.shape
    for s in range(slots):
        for j in range(rows.shape[1] // LANES):
            top = 3 * lines + j * CAPACITY
            rows[s * CAPACITY : (s + 1) * CAPACITY, j * LANES : (j + 1) * LANES] = arr_ref[
                s, top : top + CAPACITY
            ]
    writes = [pltpu.make_async_copy(rows, rows_hbm, sems.at[6])]
    writes[0].start()
    sum_experts(pc_ref, arr_ref, (s0, s1))
    for which in range(3):
        part = slice(which * lines, (which + 1) * lines)
        for e in range(experts):
            at = (e, which)
            grad = s0[e, part] + s1[e, part]
            fresh[e] = updated_master(ms[at], m1[at], m2[at], grad).astype(BF)
        if which < 2:
            for t in range(slots):
                picks[which, t] = fresh[pn_ref[t]]
            part = pick_hbm.at[:, pl.ds(which * lines, lines)]
            writes.append(pltpu.make_async_copy(picks.at[which], part, sems.at[which]))
            writes[-1].start()
    side = jnp.concatenate([fresh[e] for e in range(experts)], axis=1)
    turned[...] = dot(piece_map(), side).reshape(turned.shape)
    hid = lax.axis_index("hid")
    for k, piece_ref in enumerate((p0, p1, p2, p3)):
        mine = turned[lax.rem(hid + k, 4)]
        for e in range(experts):
            split[k, e] = mine[:, e * LANES : (e + 1) * LANES].astype(BF)
        writes.append(pltpu.make_async_copy(split.at[k], piece_ref, sems.at[2 + k]))
        writes[-1].start()
    for write in writes:
        write.wait()


def adam_pick_call(place_cur, place_next, arrived, states):
    slots = arrived.shape[0]
    experts, _, lines, _ = states[0].shape
    smem = pl.BlockSpec(memory_space=pltpu.SMEM)
    vmem = pl.BlockSpec(memory_space=pltpu.VMEM)
    rows_shape = (slots * CAPACITY, (arrived.shape[1] - 3 * lines) // CAPACITY * LANES)
    return pl.pallas_call(
        adam_pick_kernel,
        in_specs=[smem, smem] + [vmem] * 4,
        out_specs=[pl.BlockSpec(memory_space=pltpu.HBM)] * 6,
        out_shape=[pltpu.HBM((slots, 2 * lines, LANES), BF)]
        + [pltpu.HBM((experts, lines // 4, LANES), BF)] * 4
        + [pltpu.HBM(rows_shape, BF)],
        scratch_shapes=[pltpu.VMEM((experts, 3 * lines, LANES), F32)] * 2
        + [
            pltpu.VMEM((experts, lines, LANES), BF),
            pltpu.VMEM((4, lines // 4, experts * LANES), F32),
            pltpu.VMEM((2, slots, lines, LANES), BF),
            pltpu.VMEM((4, experts, lines // 4, LANES), BF),
            pltpu.VMEM(rows_shape, BF),
            pltpu.SemaphoreType.DMA((7,)),
        ],
        cost_estimate=pl.CostEstimate(flops=20 << 20, bytes_accessed=6 << 20, transcendentals=0),
        compiler_params=limits(10),
        name="adam_pick",
    )(place_cur, place_next, arrived, *states)


def adam_full_kernel(pc_ref, arr_ref, ms, m1, m2, *refs):
    om, o1, o2, s0, s1 = refs[-5:]
    sum_experts(pc_ref, arr_ref, (s0, s1))
    for e in range(ms.shape[0]):
        om[e, 0], o1[e, 0], o2[e, 0] = adam_update(ms[e, 0], m1[e, 0], m2[e, 0], s0[e] + s1[e])


def adam_full_call(place_cur, arrived, states, first, count, held):
    slots = arrived.shape[0]
    experts, _, lines, _ = states[0].shape
    state = pl.BlockSpec((experts, 1, lines, LANES), lambda i: (0, first + i, 0, 0))
    return pl.pallas_call(
        adam_full_kernel,
        grid=(count,),
        in_specs=[
            pl.BlockSpec(memory_space=pltpu.SMEM),
            pl.BlockSpec((slots, lines, LANES), lambda i: (0, first + i, 0)),
            state, state, state,
        ]
        + [pl.BlockSpec(memory_space=pl.ANY)] * len(held),
        out_specs=[state, state, state],
        out_shape=[jax.ShapeDtypeStruct(s.shape, F32) for s in states],
        scratch_shapes=[pltpu.VMEM((experts, lines, LANES), F32)] * 2,
        input_output_aliases={5 + k: k for k in range(len(held))},
        cost_estimate=pl.CostEstimate(flops=20 << 20, bytes_accessed=6 << 20, transcendentals=0),
        compiler_params=limits(60),
    )(place_cur, arrived, *states, *held)


def pick_kernel(pn_ref, p0, p1, p2, p3, out_ref):
    for t in range(out_ref.shape[0]):
        expert = pn_ref[t]
        own = [p[expert].astype(F32) for p in (p0, p1, p2, p3)]
        for a in range(3):
            out_ref[t, a * 32 : (a + 1) * 32] = jnp.concatenate(
                [v[a * 8 : (a + 1) * 8] for v in own], axis=0
            ).astype(BF)


def pick_call(place_next, pieces):
    slots = place_next.shape[0]
    shape = (slots, 4 * pieces[0].shape[1], LANES)
    return pl.pallas_call(
        pick_kernel,
        in_specs=[pl.BlockSpec(memory_space=pltpu.SMEM)] + [VM] * len(pieces),
        out_specs=VM,
        out_shape=jax.ShapeDtypeStruct(shape, BF),
        cost_estimate=pl.CostEstimate(flops=1 << 20, bytes_accessed=2 << 20, transcendentals=0),
        compiler_params=limits(4),
        name="pick",
    )(place_next, *pieces)


def hidden_kernel(w_ref, r0, r1, r2, r3, out_ref, mat):
    units = out_ref.shape[0]
    swap = swap_map(16, 16)
    for group in range(4):
        for a in range(3):
            both = jnp.concatenate(
                [
                    w_ref[group * 8 : group * 8 + 8, m * 96 + a * 32 : m * 96 + a * 32 + 32].reshape(
                        256, LANES
                    )
                    for m in range(2)
                ],
                axis=1,
            )
            turned = dot(swap, both).astype(BF)
            for m in range(2):
                top = m * units + (group * 3 + a) * 16
                for j in range(16):
                    mat[top : top + 16, j * LANES : (j + 1) * LANES] = turned[
                        j * 16 : (j + 1) * 16, m * LANES : (m + 1) * LANES
                    ]
    total = None
    for k, rows in enumerate((r0, r1, r2, r3)):
        quarter = rows.shape[1]
        turn = lax.rem(lax.axis_index("hid") + 4 - k, 4)
        start = pl.multiple_of(turn * quarter, quarter)
        term = dot(mat[:, pl.ds(start, quarter)], rows[...], NT)
        total = term if total is None else total + term
    gate, up = total[:units], total[units:]
    out_ref[...] = (gate * jax.nn.sigmoid(gate) * up).astype(BF)


def hidden_call(packed, rows):
    units = packed.shape[0] * 6
    count, quarter = rows[0].shape
    return pl.pallas_call(
        hidden_kernel,
        in_specs=[VM] * (1 + len(rows)),
        out_specs=VM,
        out_shape=jax.ShapeDtypeStruct((units, count), BF),
        scratch_shapes=[pltpu.VMEM((2 * units, 4 * quarter), BF)],
        cost_estimate=pl.CostEstimate(
            flops=16 * count * quarter * units, bytes_accessed=4 << 20, transcendentals=count * units
        ),
        compiler_params=limits(6),
        name="hidden",
    )(packed, *rows)


def unpack_kernel(w_ref, out_ref):
    swap = swap_map(16, 16)
    lines = w_ref.shape[1]
    row = lax.broadcasted_iota(jnp.int32, (256, 256), 0)
    col = lax.broadcasted_iota(jnp.int32, (256, 256), 1)
    k, j, s, b = row // 64, row // 16 % 4, row // 2 % 8, row % 2
    turn = jnp.where(col == ((s * 4 + k) * 2 + b) * 4 + j, 1.0, 0.0).astype(BF)
    for group in range(4):
        for a in range(lines // 32):
            turned = dot(
                turn, w_ref[group * 8 : group * 8 + 8, a * 32 : a * 32 + 32].reshape(256, LANES)
            ).astype(BF)
            top = (group * 3 + a) * 16
            for k in range(4):
                for j in range(4):
                    at = (k * 4 + j) * 16
                    out_ref[k, top : top + 16, j * LANES : (j + 1) * LANES] = turned[at : at + 16]


def unpack_call(packed):
    shape = (4, packed.shape[0] * 6, 4 * LANES)
    return pl.pallas_call(
        unpack_kernel,
        in_specs=[VM],
        out_specs=VM,
        out_shape=jax.ShapeDtypeStruct(shape, BF),
        cost_estimate=pl.CostEstimate(flops=1 << 28, bytes_accessed=2 << 20, transcendentals=0),
        compiler_params=limits(4),
        name="unpack",
    )(packed)


def down_kernel(w_ref, h0, h1, h2, h3, out_ref):
    total = None
    for k, h in enumerate((h0, h1, h2, h3)):
        term = dot(h[...], w_ref[k], TN)
        total = term if total is None else total + term
    out_ref[...] = total.astype(BF)


def down_call(weights, hidden):
    units, count = hidden[0].shape
    quarter = weights.shape[2]
    return pl.pallas_call(
        down_kernel,
        in_specs=[VM] * (1 + len(hidden)),
        out_specs=VM,
        out_shape=jax.ShapeDtypeStruct((count, quarter), BF),
        cost_estimate=pl.CostEstimate(
            flops=8 * count * quarter * units, bytes_accessed=3 << 20, transcendentals=0
        ),
        compiler_params=limits(4),
        name="down",
    )(weights, *hidden)


def shards(
    master,
    first_moment,
    second_moment,
    slot_weights,
    back_rows,
    readout,
    ref_logratio,
    labels,
    place_cur,
    place_next,
    fwd_rows,
    routes,
):
    slot_count = lax.axis_size("slot")
    hid_count = lax.axis_size("hid")
    _, width = back_rows.shape[1:]

    def pass_on(value, k):
        return lax.ppermute(value, "hid", [(i, (i + k) % hid_count) for i in range(hid_count)])

    def exchange(value):
        return lax.all_to_all(value, "slot", split_axis=0, concat_axis=0, tiled=True)

    capacity = CAPACITY
    quarter = fwd_rows.shape[1]
    everyone = slot_count * hid_count
    inputs, direction, a, b, h, part, sent, slot_place = scores_call(
        back_rows[0], readout[0], slot_weights.reshape(-1, width), ref_logratio,
        routes.reshape(1, -1), fwd_rows, everyone,
    )
    parts = lax.all_to_all(part, ("slot", "hid"), split_axis=0, concat_axis=0, tiled=True)
    blocks = grads_call(
        parts, labels.reshape(part.shape[1:]), a, b, h, sent, direction, inputs, slot_count
    )
    arrived = exchange(blocks)

    lines = 96
    shape = (master.shape[0], 3, lines, LANES)
    states = [v.reshape(shape) for v in (master, first_moment, second_moment)]
    picked, *pieces, own_rows = adam_pick_call(place_cur, place_next, arrived, states)
    far_rows = pass_on(own_rows, 2)
    all_rows = [own_rows, pass_on(own_rows, 1), far_rows, pass_on(own_rows, 3)]

    gate_up = in_hbm(exchange(picked))
    pieces = [pieces[0]] + [pass_on(pieces[k], k) for k in range(1, hid_count)]
    down = pick_call(place_next, pieces)
    down = exchange(down)

    held = adam_full_call(place_cur, arrived, states, 0, 2, [])
    held = adam_full_call(place_cur, arrived, states, 2, 1, held)

    hidden = hidden_call(gate_up, all_rows)
    far_hidden = pass_on(hidden, 2)
    hidden = [hidden, pass_on(hidden, 1), far_hidden, pass_on(hidden, 3)]
    produced = down_call(unpack_call(down), hidden)
    returned = exchange(produced.reshape(slot_count, capacity, quarter))
    place_map = (
        slot_place == jnp.arange(slot_count * capacity, dtype=jnp.int32)[:, None]
    ).astype(BF)
    out_rows = lax.dot_general(
        place_map,
        returned.reshape(slot_count * capacity, quarter),
        (((0,), (0,)), ((), ())),
        preferred_element_type=F32,
    ).astype(BF)
    return (out_rows, *[v.reshape(master.shape) for v in held])


def solution(mesh):
    shard = P(None, None, "hid", "slot")
    return jax.shard_map(
        shards,
        mesh=mesh,
        in_specs=(
            shard,
            shard,
            shard,
            P("slot", None, "hid", None),
            P("slot", None, None),
            P("slot", None, None),
            P("slot", None),
            P("slot", None),
            P(),
            P(),
            P("slot", "hid"),
            P("slot", None),
        ),
        out_specs=(P("slot", "hid"), shard, shard, shard),
        check_vma=False,
    )
```

```python
import jax
import jax.numpy as jnp
from jax import lax
from jax.experimental import pallas as pl
from jax.experimental.pallas import tpu as pltpu
from jax.sharding import PartitionSpec as P

desired_weight = 1.0
undesired_weight = 1.33
learn_rate = 0.004
decay_first = 0.9
decay_second = 0.999
correct_first = 0.9999734386011124
correct_second = 0.09520785288629043
adam_eps = 1e-08
weight_decay = 0.1

BF = jnp.bfloat16
F32 = jnp.float32
NT = (((1,), (1,)), ((), ()))
TN = (((0,), (0,)), ((), ()))
LANES = 128
CAPACITY = 16
CHUNKS = 2
AHEAD = 3


def dot(a, b, dims=(((1,), (0,)), ((), ()))):
    return lax.dot_general(a, b, dims, preferred_element_type=F32)


def swap_map(first, second, tail=1):
    size = first * second * tail
    row = lax.broadcasted_iota(jnp.int32, (size, size), 0)
    col = lax.broadcasted_iota(jnp.int32, (size, size), 1)
    b, a, t = row // (first * tail), row // tail % first, row % tail
    return jnp.where(col == (a * second + b) * tail + t, 1.0, 0.0).astype(BF)


def piece_map():
    row = lax.broadcasted_iota(jnp.int32, (96, 96), 0)
    col = lax.broadcasted_iota(jnp.int32, (96, 96), 1)
    q, unit, j = row // 24, row // 4 % 6, row % 4
    return jnp.where(col == (unit * 4 + q) * 4 + j, 1.0, 0.0).astype(BF)


VM = pl.BlockSpec(memory_space=pltpu.VMEM)


def in_hbm(value):
    return pltpu.with_memory_space_constraint(value, pltpu.HBM)


def limits(mib):
    return pltpu.CompilerParams(vmem_limit_bytes=mib << 20)


def scores_kernel(
    x_hbm, r_hbm, w_hbm, log_ref, route_ref, fwd_ref,
    x_ref, r_ref, a_ref, b_ref, h_ref, parts_ref, sent_ref, place_ref, w_ref, sems,
):
    rows = x_ref.shape[0]
    units = h_ref.shape[0]
    block = rows // CHUNKS
    pairs = [(w_hbm.at[pl.ds(0, 2 * units)], w_ref.at[pl.ds(0, 2 * units)])]
    for c in range(CHUNKS):
        part = pl.ds(c * block, block)
        pairs.append((x_hbm.at[part], x_ref.at[part]))
        if c == 0:
            down = pl.ds(2 * units, units)
            pairs.append((w_hbm.at[down], w_ref.at[down]))
        pairs.append((r_hbm.at[part], r_ref.at[part]))
    copies = [pltpu.make_async_copy(*pair, sems.at[k]) for k, pair in enumerate(pairs)]

    def arrive(k):
        copies[k].wait()
        if k + AHEAD < len(copies):
            copies[k + AHEAD].start()

    for copy in copies[:AHEAD]:
        copy.start()

    count = fwd_ref.shape[0]
    span = sent_ref.shape[0]
    slots = 2 * count // CAPACITY
    route = route_ref[...]
    named = route == lax.broadcasted_iota(jnp.int32, (slots, count), 0)
    before = lax.broadcasted_iota(jnp.int32, (count, count), 0) < lax.broadcasted_iota(
        jnp.int32, (count, count), 1
    )
    earlier = dot(jnp.where(named, 1.0, 0.0).astype(BF), jnp.where(before, 1.0, 0.0).astype(BF))
    position = jnp.sum(jnp.where(named, earlier, 0.0), axis=0, keepdims=True)
    place = route * CAPACITY + position.astype(jnp.int32)
    place_ref[...] = place
    hit = place == lax.broadcasted_iota(jnp.int32, (span, count), 0)
    sent_ref[...] = dot(jnp.where(hit, 1.0, 0.0).astype(BF), fwd_ref[...]).astype(BF)

    arrive(0)
    terms = []
    for c in range(CHUNKS):
        cols = slice(c * block, (c + 1) * block)
        arrive(2 * c + 1 + (c > 0))
        both = dot(w_ref[0 : 2 * units], x_ref[cols], NT)
        if c == 0:
            arrive(2)
        arrive(2 * c + 3)
        dh = dot(w_ref[2 * units :], r_ref[cols], NT)
        gate, up = both[:units], both[units:]
        sigma = jax.nn.sigmoid(gate)
        hidden = (gate * sigma * up).astype(BF)
        h_ref[:, cols] = hidden
        term = jnp.sum(hidden.astype(F32) * dh, axis=0, keepdims=True) - 0.25 * log_ref[:, cols]
        terms += [term[:, k * LANES : (k + 1) * LANES] for k in range(block // LANES)]
        a_ref[:, cols] = dh * up * sigma * (1.0 + gate * (1.0 - sigma))
        b_ref[:, cols] = dh * gate * sigma
    term = jnp.concatenate(terms, axis=0)
    for k in range(parts_ref.shape[0]):
        parts_ref[k] = term


def scores_call(inputs, direction, weights, ref_logratio, route, fwd_rows, everyone):
    rows, width = inputs.shape
    units = weights.shape[0] // 3
    span = 2 * fwd_rows.shape[0]
    hbm = pl.BlockSpec(memory_space=pltpu.HBM)
    vmem = pl.BlockSpec(memory_space=pltpu.VMEM)
    return pl.pallas_call(
        scores_kernel,
        in_specs=[hbm, hbm, hbm, vmem, vmem, vmem],
        out_specs=[vmem] * 8,
        out_shape=[
            pltpu.VMEM((rows, width), BF),
            pltpu.VMEM((rows, width), BF),
            pltpu.VMEM((units, rows), F32),
            pltpu.VMEM((units, rows), F32),
            pltpu.VMEM((units, rows), BF),
            jax.ShapeDtypeStruct((everyone, rows // LANES, LANES), F32),
            pltpu.VMEM((span, fwd_rows.shape[1]), BF),
            jax.ShapeDtypeStruct((1, fwd_rows.shape[0]), jnp.int32),
        ],
        scratch_shapes=[
            pltpu.VMEM(weights.shape, BF),
            pltpu.SemaphoreType.DMA((2 * CHUNKS + 2,)),
        ],
        cost_estimate=pl.CostEstimate(
            flops=6 * rows * width * units, bytes_accessed=14 << 20, transcendentals=rows * units
        ),
        compiler_params=limits(48),
        name="scores",
    )(inputs, direction, weights, ref_logratio, route, fwd_rows)


def grads_kernel(parts_ref, lab_ref, a_ref, b_ref, h_ref, sent_ref, r_ref, x_ref, out_ref, lhs, held):
    units, rows = a_ref.shape
    wide = 512
    slots = out_ref.shape[0]
    center = jnp.sum(parts_ref[...]) / (slots * rows)
    hids = parts_ref.shape[0] // slots
    q = jax.nn.sigmoid(jnp.sum(parts_ref[pl.ds(lax.axis_index("slot") * hids, hids)], axis=0) - center)
    slope = q * (1.0 - q) * jnp.where(lab_ref[...] == 1, -desired_weight, undesired_weight)
    for k, term in enumerate((a_ref, b_ref, h_ref)):
        for i in range(rows // LANES):
            cols = slice(i * LANES, (i + 1) * LANES)
            lhs[k * units : (k + 1) * units, cols] = (
                term[:, cols].astype(F32) * slope[i : i + 1]
            ).astype(BF)

    @pl.loop(0, x_ref.shape[1] // wide)
    def _(step):
        cols = pl.ds(pl.multiple_of(step * wide, wide), wide)
        held[0 : 2 * units, cols] = dot(lhs[0 : 2 * units], x_ref[:, cols]).astype(BF)
        held[2 * units :, cols] = dot(lhs[2 * units :], r_ref[:, cols]).astype(BF)

    swap = swap_map(16, 16)
    for k in range(3):
        for pair in range(units // 32):
            halves = []
            for half in range(2):
                base = k * units + (2 * pair + half) * 16
                tiles = [held[base : base + 16, j * LANES : (j + 1) * LANES] for j in range(16)]
                halves.append(jnp.concatenate(tiles, axis=0))
            both = dot(swap, jnp.concatenate(halves, axis=1)).astype(BF)
            for half in range(2):
                for p in range(8):
                    at = (2 * pair + half) * 256 + p * 32
                    top = k * 96 + at % 96
                    out_ref[at // 96, top : top + 32] = both[
                        p * 32 : (p + 1) * 32, half * LANES : (half + 1) * LANES
                    ]
    for s in range(slots):
        for j in range(sent_ref.shape[1] // LANES):
            top = 288 + j * CAPACITY
            out_ref[s, top : top + CAPACITY] = sent_ref[
                s * CAPACITY : (s + 1) * CAPACITY, j * LANES : (j + 1) * LANES
            ]


def grads_call(parts, labels, a, b, h, sent, direction, inputs, slots):
    units, rows = a.shape
    width = inputs.shape[1]
    vmem = pl.BlockSpec(memory_space=pltpu.VMEM)
    return pl.pallas_call(
        grads_kernel,
        in_specs=[vmem] * 8,
        out_specs=vmem,
        out_shape=jax.ShapeDtypeStruct((slots, 288 + 4 * CAPACITY, LANES), BF),
        scratch_shapes=[pltpu.VMEM((3 * units, rows), BF), pltpu.VMEM((3 * units, width), BF)],
        cost_estimate=pl.CostEstimate(
            flops=6 * rows * width * units, bytes_accessed=12 << 20, transcendentals=rows
        ),
        compiler_params=limits(6),
        name="grads",
    )(parts, labels, a, b, h, sent, direction, inputs)


def adam_update(master, first, second, grad):
    new_first = decay_first * first + (1.0 - decay_first) * grad
    new_second = decay_second * second + (1.0 - decay_second) * grad * grad
    size = jnp.sqrt(new_second * (1.0 / correct_second)) + adam_eps
    update = new_first * (1.0 / correct_first) / size
    return master - learn_rate * (update + weight_decay * master), new_first, new_second


def updated_master(master, first, second, grad):
    step = (learn_rate * decay_first / correct_first) * first + (
        learn_rate * (1.0 - decay_first) / correct_first
    ) * grad
    second = (decay_second / correct_second) * second + (
        (1.0 - decay_second) / correct_second
    ) * (grad * grad)
    size = second * lax.rsqrt(second) + adam_eps
    return (1.0 - learn_rate * weight_decay) * master - step / size


def sum_experts(pc_ref, arr_ref, sums):
    lines = sums[0].shape[1]
    for part in sums:
        part[...] = jnp.zeros_like(part)
    for s in range(arr_ref.shape[0]):
        sums[s % len(sums)][pc_ref[s]] += arr_ref[s, 0:lines].astype(F32)


def adam_pick_kernel(
    pc_ref, pn_ref, arr_ref, ms, m1, m2,
    pick_hbm, p0, p1, p2, p3, rows_hbm, s0, s1, fresh, turned, picks, split, rows, sems,
):
    slots = arr_ref.shape[0]
    experts, _, lines, _ = ms.shape
    for s in range(slots):
        for j in range(rows.shape[1] // LANES):
            top = 3 * lines + j * CAPACITY
            rows[s * CAPACITY : (s + 1) * CAPACITY, j * LANES : (j + 1) * LANES] = arr_ref[
                s, top : top + CAPACITY
            ]
    writes = [pltpu.make_async_copy(rows, rows_hbm, sems.at[6])]
    writes[0].start()
    sum_experts(pc_ref, arr_ref, (s0, s1))
    for which in range(3):
        part = slice(which * lines, (which + 1) * lines)
        for e in range(experts):
            at = (e, which)
            grad = s0[e, part] + s1[e, part]
            fresh[e] = updated_master(ms[at], m1[at], m2[at], grad).astype(BF)
        if which < 2:
            for t in range(slots):
                picks[which, t] = fresh[pn_ref[t]]
            part = pick_hbm.at[:, pl.ds(which * lines, lines)]
            writes.append(pltpu.make_async_copy(picks.at[which], part, sems.at[which]))
            writes[-1].start()
    side = jnp.concatenate([fresh[e] for e in range(experts)], axis=1)
    turned[...] = dot(piece_map(), side).reshape(turned.shape)
    hid = lax.axis_index("hid")
    for k, piece_ref in enumerate((p0, p1, p2, p3)):
        mine = turned[lax.rem(hid + k, 4)]
        for e in range(experts):
            split[k, e] = mine[:, e * LANES : (e + 1) * LANES].astype(BF)
        writes.append(pltpu.make_async_copy(split.at[k], piece_ref, sems.at[2 + k]))
        writes[-1].start()
    for write in writes:
        write.wait()


def adam_pick_call(place_cur, place_next, arrived, states):
    slots = arrived.shape[0]
    experts, _, lines, _ = states[0].shape
    smem = pl.BlockSpec(memory_space=pltpu.SMEM)
    vmem = pl.BlockSpec(memory_space=pltpu.VMEM)
    rows_shape = (slots * CAPACITY, (arrived.shape[1] - 3 * lines) // CAPACITY * LANES)
    return pl.pallas_call(
        adam_pick_kernel,
        in_specs=[smem, smem] + [vmem] * 4,
        out_specs=[pl.BlockSpec(memory_space=pltpu.HBM)] * 6,
        out_shape=[pltpu.HBM((slots, 2 * lines, LANES), BF)]
        + [pltpu.HBM((experts, lines // 4, LANES), BF)] * 4
        + [pltpu.HBM(rows_shape, BF)],
        scratch_shapes=[pltpu.VMEM((experts, 3 * lines, LANES), F32)] * 2
        + [
            pltpu.VMEM((experts, lines, LANES), BF),
            pltpu.VMEM((4, lines // 4, experts * LANES), F32),
            pltpu.VMEM((2, slots, lines, LANES), BF),
            pltpu.VMEM((4, experts, lines // 4, LANES), BF),
            pltpu.VMEM(rows_shape, BF),
            pltpu.SemaphoreType.DMA((7,)),
        ],
        cost_estimate=pl.CostEstimate(flops=20 << 20, bytes_accessed=6 << 20, transcendentals=0),
        compiler_params=limits(10),
        name="adam_pick",
    )(place_cur, place_next, arrived, *states)


def adam_full_kernel(pc_ref, arr_ref, ms, m1, m2, *refs):
    om, o1, o2, s0, s1 = refs[-5:]
    sum_experts(pc_ref, arr_ref, (s0, s1))
    for e in range(ms.shape[0]):
        om[e, 0], o1[e, 0], o2[e, 0] = adam_update(ms[e, 0], m1[e, 0], m2[e, 0], s0[e] + s1[e])


def adam_full_call(place_cur, arrived, states, first, count, held):
    slots = arrived.shape[0]
    experts, _, lines, _ = states[0].shape
    parts = 2 if count == 1 else 1
    block = lines // parts
    state = pl.BlockSpec(
        (experts, 1, block, LANES), lambda i: (0, first + i // parts, i % parts, 0)
    )
    return pl.pallas_call(
        adam_full_kernel,
        grid=(parts * count,),
        in_specs=[
            pl.BlockSpec(memory_space=pltpu.SMEM),
            pl.BlockSpec((slots, block, LANES), lambda i: (0, parts * first + i, 0)),
            state, state, state,
        ]
        + [pl.BlockSpec(memory_space=pl.ANY)] * len(held),
        out_specs=[state, state, state],
        out_shape=[jax.ShapeDtypeStruct(s.shape, F32) for s in states],
        scratch_shapes=[pltpu.VMEM((experts, block, LANES), F32)] * 2,
        input_output_aliases={5 + k: k for k in range(len(held))},
        cost_estimate=pl.CostEstimate(flops=20 << 20, bytes_accessed=6 << 20, transcendentals=0),
        compiler_params=limits(60),
    )(place_cur, arrived, *states, *held)


def pick_kernel(pn_ref, p0, p1, p2, p3, out_ref):
    for t in range(out_ref.shape[0]):
        expert = pn_ref[t]
        own = [p[expert].astype(F32) for p in (p0, p1, p2, p3)]
        for a in range(3):
            out_ref[t, a * 32 : (a + 1) * 32] = jnp.concatenate(
                [v[a * 8 : (a + 1) * 8] for v in own], axis=0
            ).astype(BF)


def pick_call(place_next, pieces):
    slots = place_next.shape[0]
    shape = (slots, 4 * pieces[0].shape[1], LANES)
    return pl.pallas_call(
        pick_kernel,
        in_specs=[pl.BlockSpec(memory_space=pltpu.SMEM)] + [VM] * len(pieces),
        out_specs=VM,
        out_shape=jax.ShapeDtypeStruct(shape, BF),
        cost_estimate=pl.CostEstimate(flops=1 << 20, bytes_accessed=2 << 20, transcendentals=0),
        compiler_params=limits(4),
        name="pick",
    )(place_next, *pieces)


def hidden_kernel(w_ref, r0, r1, r2, r3, out_ref, mat):
    units = out_ref.shape[0]
    swap = swap_map(16, 16)
    for group in range(4):
        for a in range(3):
            both = jnp.concatenate(
                [
                    w_ref[group * 8 : group * 8 + 8, m * 96 + a * 32 : m * 96 + a * 32 + 32].reshape(
                        256, LANES
                    )
                    for m in range(2)
                ],
                axis=1,
            )
            turned = dot(swap, both).astype(BF)
            for m in range(2):
                top = m * units + (group * 3 + a) * 16
                for j in range(16):
                    mat[top : top + 16, j * LANES : (j + 1) * LANES] = turned[
                        j * 16 : (j + 1) * 16, m * LANES : (m + 1) * LANES
                    ]
    total = None
    for k, rows in enumerate((r0, r1, r2, r3)):
        quarter = rows.shape[1]
        turn = lax.rem(lax.axis_index("hid") + 4 - k, 4)
        start = pl.multiple_of(turn * quarter, quarter)
        term = dot(mat[:, pl.ds(start, quarter)], rows[...], NT)
        total = term if total is None else total + term
    gate, up = total[:units], total[units:]
    out_ref[...] = (gate * jax.nn.sigmoid(gate) * up).astype(BF)


def hidden_call(packed, rows):
    units = packed.shape[0] * 6
    count, quarter = rows[0].shape
    return pl.pallas_call(
        hidden_kernel,
        in_specs=[VM] * (1 + len(rows)),
        out_specs=VM,
        out_shape=jax.ShapeDtypeStruct((units, count), BF),
        scratch_shapes=[pltpu.VMEM((2 * units, 4 * quarter), BF)],
        cost_estimate=pl.CostEstimate(
            flops=16 * count * quarter * units, bytes_accessed=4 << 20, transcendentals=count * units
        ),
        compiler_params=limits(6),
        name="hidden",
    )(packed, *rows)


def unpack_kernel(w_ref, out_ref):
    swap = swap_map(16, 16)
    lines = w_ref.shape[1]
    row = lax.broadcasted_iota(jnp.int32, (256, 256), 0)
    col = lax.broadcasted_iota(jnp.int32, (256, 256), 1)
    k, j, s, b = row // 64, row // 16 % 4, row // 2 % 8, row % 2
    turn = jnp.where(col == ((s * 4 + k) * 2 + b) * 4 + j, 1.0, 0.0).astype(BF)
    for group in range(4):
        for a in range(lines // 32):
            turned = dot(
                turn, w_ref[group * 8 : group * 8 + 8, a * 32 : a * 32 + 32].reshape(256, LANES)
            ).astype(BF)
            top = (group * 3 + a) * 16
            for k in range(4):
                for j in range(4):
                    at = (k * 4 + j) * 16
                    out_ref[k, top : top + 16, j * LANES : (j + 1) * LANES] = turned[at : at + 16]


def unpack_call(packed):
    shape = (4, packed.shape[0] * 6, 4 * LANES)
    return pl.pallas_call(
        unpack_kernel,
        in_specs=[VM],
        out_specs=VM,
        out_shape=jax.ShapeDtypeStruct(shape, BF),
        cost_estimate=pl.CostEstimate(flops=1 << 28, bytes_accessed=2 << 20, transcendentals=0),
        compiler_params=limits(4),
        name="unpack",
    )(packed)


def down_kernel(w_ref, h0, h1, h2, h3, out_ref):
    total = None
    for k, h in enumerate((h0, h1, h2, h3)):
        term = dot(h[...], w_ref[k], TN)
        total = term if total is None else total + term
    out_ref[...] = total.astype(BF)


def down_call(weights, hidden):
    units, count = hidden[0].shape
    quarter = weights.shape[2]
    return pl.pallas_call(
        down_kernel,
        in_specs=[VM] * (1 + len(hidden)),
        out_specs=VM,
        out_shape=jax.ShapeDtypeStruct((count, quarter), BF),
        cost_estimate=pl.CostEstimate(
            flops=8 * count * quarter * units, bytes_accessed=3 << 20, transcendentals=0
        ),
        compiler_params=limits(4),
        name="down",
    )(weights, *hidden)


def shards(
    master,
    first_moment,
    second_moment,
    slot_weights,
    back_rows,
    readout,
    ref_logratio,
    labels,
    place_cur,
    place_next,
    fwd_rows,
    routes,
):
    slot_count = lax.axis_size("slot")
    hid_count = lax.axis_size("hid")
    _, width = back_rows.shape[1:]

    def pass_on(value, k):
        return lax.ppermute(value, "hid", [(i, (i + k) % hid_count) for i in range(hid_count)])

    def exchange(value):
        return lax.all_to_all(value, "slot", split_axis=0, concat_axis=0, tiled=True)

    capacity = CAPACITY
    quarter = fwd_rows.shape[1]
    everyone = slot_count * hid_count
    inputs, direction, a, b, h, part, sent, slot_place = scores_call(
        back_rows[0], readout[0], slot_weights.reshape(-1, width), ref_logratio,
        routes.reshape(1, -1), fwd_rows, everyone,
    )
    parts = lax.all_to_all(part, ("slot", "hid"), split_axis=0, concat_axis=0, tiled=True)
    blocks = grads_call(
        parts, labels.reshape(part.shape[1:]), a, b, h, sent, direction, inputs, slot_count
    )
    arrived = exchange(blocks)

    lines = 96
    shape = (master.shape[0], 3, lines, LANES)
    states = [v.reshape(shape) for v in (master, first_moment, second_moment)]
    picked, *pieces, own_rows = adam_pick_call(place_cur, place_next, arrived, states)
    far_rows = pass_on(own_rows, 2)
    all_rows = [own_rows, pass_on(own_rows, 1), far_rows, pass_on(own_rows, 3)]

    gate_up = in_hbm(exchange(picked))
    pieces = [pieces[0]] + [pass_on(pieces[k], k) for k in range(1, hid_count)]
    down = pick_call(place_next, pieces)
    down = exchange(down)

    held = adam_full_call(place_cur, arrived, states, 0, 2, [])
    held = adam_full_call(place_cur, arrived, states, 2, 1, held)

    hidden = hidden_call(gate_up, all_rows)
    far_hidden = pass_on(hidden, 2)
    hidden = [hidden, pass_on(hidden, 1), far_hidden, pass_on(hidden, 3)]
    produced = down_call(unpack_call(down), hidden)
    returned = exchange(produced.reshape(slot_count, capacity, quarter))
    place_map = (
        slot_place == jnp.arange(slot_count * capacity, dtype=jnp.int32)[:, None]
    ).astype(BF)
    out_rows = lax.dot_general(
        place_map,
        returned.reshape(slot_count * capacity, quarter),
        (((0,), (0,)), ((), ())),
        preferred_element_type=F32,
    ).astype(BF)
    return (out_rows, *[v.reshape(master.shape) for v in held])


def solution(mesh):
    shard = P(None, None, "hid", "slot")
    return jax.shard_map(
        shards,
        mesh=mesh,
        in_specs=(
            shard,
            shard,
            shard,
            P("slot", None, "hid", None),
            P("slot", None, None),
            P("slot", None, None),
            P("slot", None),
            P("slot", None),
            P(),
            P(),
            P("slot", "hid"),
            P("slot", None),
        ),
        out_specs=(P("slot", "hid"), shard, shard, shard),
        check_vma=False,
    )
```
